32 devices in a mesh: groups: 2 (over y), rows: 16 (over z, x, core).
Axes of the slice: x: 2, y: 2, z: 4, core: 2. Of those that a mesh axis runs over, the one named last changes fastest.
Arguments:
- scene_map: bfloat16 [128, 128, 1024], P(('groups', 'rows')), parts along dimension 0, may hold values from -6 to 6
- reduce_kernel: bfloat16 [128, 8, 32], replicated, may hold values from -0.25 to 0.25
- reduce_bias: float32 [32], replicated, may hold values from -3 to 3
- spatial_kernel: bfloat16 [9, 32, 8, 32], replicated, may hold values from -0.1875 to 0.1875
- spatial_bias: float32 [32], replicated, may hold values from -3 to 3
- widen_kernel: bfloat16 [32, 8, 128], replicated, may hold values from -0.5 to 0.5
- widen_bias: float32 [128], replicated, may hold values from -3 to 3
- entry_kernel: bfloat16 [128, 8, 64], replicated, may hold values from -0.25 to 0.25
- entry_bias: float32 [64], replicated, may hold values from -3 to 3
- stride_kernel: bfloat16 [9, 64, 8, 64], replicated, may hold values from -0.125 to 0.125
- stride_bias: float32 [64], replicated, may hold values from -3 to 3
Outputs:
- section_three: bfloat16 [128, 128, 1024], P(('groups', 'rows')), parts along dimension 0
- section_four: bfloat16 [64, 64, 512], P(('groups', 'rows')), parts along dimension 0
The draws below stay inside these ranges and needn't reach their ends.
There are 2 independent parts, one for each index of `groups`. The reference program is written for one: setup_inputs(seed, part) draws one part's arguments, and reference() takes and returns one part's arrays. A program takes and returns all parts, laid end to end along the dimension named above; an argument that names none is the same for every part. Nothing has to cross between parts.
All inputs are finite; a program needn't handle non-finite values.
Results may differ from the reference program's by a relative error of at most 0.0095.
Values may be sent and summed in bfloat16 or wider, within the bound.
No kernel may reach another device: no remote copies, remote signals or barrier semaphores. Data moves between devices by JAX's collectives and lax.ppermute only.
A program may use at most 192 MiB of HBM per device.

```python
import jax
import jax.numpy as jnp
import numpy as np

IN_F = 128
MID_F = 32
S4_F = 64
ORIENT = 8
COLS = 128
HEIGHT = 64


def block_scale(own_key, extent, cuts, smallest, top_value):
    def one(position, parts):
        heights = jax.random.uniform(jax.random.fold_in(jax.random.fold_in(own_key, 6), position), (parts,), jnp.float32, smallest / len(cuts), top_value / len(cuts))
        return jnp.repeat(jnp.exp(heights), extent[position] // parts).reshape((-1,) + (1,) * (len(extent) - position - 1))

    loudness = one(*cuts[0])
    for cut in cuts[1:]:
        loudness = loudness * one(*cut)
    return loudness


def bell_draw(rng, extent, width, most, pieces=(), dtype=jnp.bfloat16):
    factor_of = block_scale(rng, extent, pieces, -0.22, 0.18) if pieces else 1.0
    result = jax.random.normal(rng, extent, jnp.float32) * width * factor_of
    return jnp.minimum(jnp.maximum(result, -most), most).astype(dtype)


def setup_inputs(seed: int = 0, part: int = 0) -> dict:
    seeds = jax.random.split(jax.random.key(seed), 12)
    own_keys = jax.random.split(jax.random.fold_in(seeds[11], part), 12)
    scene_map = bell_draw(own_keys[0], (HEIGHT, COLS, IN_F * ORIENT), 1.0, 6.0, ((0, 16),))
    reduce_kernel = bell_draw(seeds[1], (IN_F, ORIENT, MID_F), (IN_F * ORIENT // 2) ** -0.5, 0.25)
    reduce_bias = bell_draw(seeds[2], (MID_F,), 0.5, 3.0, (), jnp.float32)
    spatial_kernel = bell_draw(seeds[3], (9, MID_F, ORIENT, MID_F), (9 * MID_F * ORIENT // 2) ** -0.5, 0.1875)
    spatial_bias = bell_draw(seeds[4], (MID_F,), 0.5, 3.0, (), jnp.float32)
    widen_kernel = bell_draw(seeds[5], (MID_F, ORIENT, IN_F), (MID_F * ORIENT // 2) ** -0.5, 0.5)
    widen_bias = bell_draw(seeds[6], (IN_F,), 0.5, 3.0, (), jnp.float32)
    entry_kernel = bell_draw(seeds[7], (IN_F, ORIENT, S4_F), (IN_F * ORIENT // 2) ** -0.5, 0.25)
    entry_bias = bell_draw(seeds[8], (S4_F,), 0.5, 3.0, (), jnp.float32)
    stride_kernel = bell_draw(seeds[9], (9, S4_F, ORIENT, S4_F), (9 * S4_F * ORIENT // 2) ** -0.5, 0.125)
    stride_bias = bell_draw(seeds[10], (S4_F,), 0.5, 3.0, (), jnp.float32)
    return dict(scene_map=scene_map, reduce_kernel=reduce_kernel, reduce_bias=reduce_bias, spatial_kernel=spatial_kernel, spatial_bias=spatial_bias, widen_kernel=widen_kernel, widen_bias=widen_bias, entry_kernel=entry_kernel, entry_bias=entry_bias, stride_kernel=stride_kernel, stride_bias=stride_bias)


CYCLE_TAPS = [0, 1, 2, 5, 8, 7, 6, 3]


def turned_taps(turn_index):
    tap_table = np.arange(9)
    for cycle_pos in range(8):
        tap_table[CYCLE_TAPS[cycle_pos]] = CYCLE_TAPS[(cycle_pos - turn_index) % 8]
    return tap_table


def unfold_group(kernel):
    tap_count = kernel.shape[0]
    in_fields, orients, out_fields = kernel.shape[1], kernel.shape[2], kernel.shape[3]
    turned = []
    for turn_index in range(orients):
        source = kernel[turned_taps(turn_index)] if tap_count == 9 else kernel
        turned.append(jnp.roll(source, turn_index, axis=2))
    stacked = jnp.stack(turned, axis=-1)
    return stacked.reshape(tap_count, in_fields * orients, out_fields * orients)


def bias_row(bias_vec):
    return jnp.repeat(bias_vec, ORIENT)


def pointwise(feature, weight):
    flattened = feature.reshape(-1, feature.shape[-1])
    product = jnp.dot(flattened, weight, preferred_element_type=jnp.float32)
    return product.reshape(feature.shape[:-1] + (weight.shape[-1],))


def stencil(feature, weight):
    row_count, col_count = feature.shape[0], feature.shape[1]
    padded = jnp.pad(feature, ((1, 1), (1, 1), (0, 0)))
    running = jnp.zeros((row_count, col_count, weight.shape[-1]), jnp.float32)
    for row_off in range(3):
        for col_off in range(3):
            window_rows = padded[row_off:row_off + row_count, col_off:col_off + col_count]
            running = running + pointwise(window_rows, weight[row_off * 3 + col_off])
    return running


def strided(feature, weight):
    out_rows, out_cols = feature.shape[0] // 2, feature.shape[1] // 2
    padded = jnp.pad(feature, ((1, 0), (1, 0), (0, 0)))
    running = jnp.zeros((out_rows, out_cols, weight.shape[-1]), jnp.float32)
    for row_off in range(3):
        for col_off in range(3):
            window_rows = padded[row_off:row_off + 2 * out_rows - 1:2, col_off:col_off + 2 * out_cols - 1:2]
            running = running + pointwise(window_rows, weight[row_off * 3 + col_off])
    return running


def reference(scene_map, reduce_kernel, reduce_bias, spatial_kernel, spatial_bias, widen_kernel, widen_bias, entry_kernel, entry_bias, stride_kernel, stride_bias):
    w_reduce = unfold_group(reduce_kernel[None])[0]
    w_spatial = unfold_group(spatial_kernel)
    w_widen = unfold_group(widen_kernel[None])[0]
    w_entry = unfold_group(entry_kernel[None])[0]
    w_stride = unfold_group(stride_kernel)
    mid_one = jax.nn.relu(pointwise(scene_map, w_reduce) + bias_row(reduce_bias)).astype(jnp.bfloat16)
    mid_two = jax.nn.relu(stencil(mid_one, w_spatial) + bias_row(spatial_bias)).astype(jnp.bfloat16)
    section_three = jax.nn.relu(scene_map.astype(jnp.float32) + pointwise(mid_two, w_widen) + bias_row(widen_bias)).astype(jnp.bfloat16)
    mid_four = jax.nn.relu(pointwise(section_three, w_entry) + bias_row(entry_bias)).astype(jnp.bfloat16)
    section_four = jax.nn.relu(strided(mid_four, w_stride) + bias_row(stride_bias)).astype(jnp.bfloat16)
    return section_three, section_four
```

```python
import functools

import jax
import jax.numpy as jnp
from jax import lax
from jax.experimental import pallas as pl
from jax.experimental.pallas import tpu as pltpu
from jax.sharding import PartitionSpec as P

ORIENT = 8
CYCLE_TAPS = [0, 1, 2, 5, 8, 7, 6, 3]
BF16, F32 = jnp.bfloat16, jnp.float32
NT = (((1,), (1,)), ((), ()))


def back_tap(tap, turn):
    if tap == 4:
        return 4
    return CYCLE_TAPS[(CYCLE_TAPS.index(tap) - turn) % ORIENT]


def iota(shape, dim):
    return lax.broadcasted_iota(jnp.int32, shape, dim)


def dot(a, b):
    return jnp.dot(a, b, preferred_element_type=F32)


def dot_nt(a, b):
    return lax.dot_general(a, b, NT, preferred_element_type=F32)


def rows_rolled(x, by):
    by %= x.shape[0]
    if by == 0:
        return x
    return jnp.concatenate([x[x.shape[0] - by:], x[:x.shape[0] - by]], 0)


def spread(fields, first, width):
    return jnp.where((iota((fields, width), 1) + first) // ORIENT == iota((fields, width), 0), 1.0, 0.0).astype(BF16)


def turned(blocks, block):
    lane = iota((1, blocks.shape[1]), 1)
    for bit in (1, 2, 4):
        take = jnp.broadcast_to(lane & bit, blocks.shape) != 0
        blocks = jnp.where(take, rows_rolled(blocks, bit * block), blocks)
    return blocks


def bias_lanes(bias, hot):
    first = bias.astype(BF16)
    rest = bias - first.astype(F32)
    second = rest.astype(BF16)
    third = (rest - second.astype(F32)).astype(BF16)
    parts = [dot(jnp.broadcast_to(p, (16,) + p.shape[1:]), hot)[:1] for p in (first, second, third)]
    return parts[0] + parts[1] + parts[2]


def unfold_kernel(kr_ref, ks_ref, kw_ref, ke_ref, kt_ref,
                  wr_ref, ws_ref, ww_ref, we_ref, k2_ref,
                  ks_v, kt_v, flat_w, flat_s, flat_t, sem):
    copy_s = pltpu.make_async_copy(ks_ref, ks_v, sem.at[0])
    copy_t = pltpu.make_async_copy(kt_ref, kt_v, sem.at[1])
    copy_s.start()
    copy_t.start()
    in_f, mid, s4 = kr_ref.shape[2], kr_ref.shape[1], ke_ref.shape[1]
    wide = in_f * ORIENT
    kr = kr_ref[...].reshape(ORIENT * mid, in_f)
    ke = ke_ref[...].reshape(ORIENT * s4, in_f)
    back = lambda x, block: jnp.concatenate([x[(-r) % ORIENT * block:((-r) % ORIENT + 1) * block] for r in range(ORIENT)], 0)
    kr, ke = back(kr, mid), back(ke, s4)
    flat_w[...] = kw_ref[...].astype(F32).reshape(mid * ORIENT, in_f)
    kw = jnp.concatenate([flat_w[pl.ds(u, mid, stride=ORIENT), :] for u in range(ORIENT)], 0).astype(BF16)
    step = 256
    for first in range(0, wide, step):
        hot = spread(in_f, first, step)
        cols = pl.ds(first, step)
        wr_ref[:, cols] = turned(dot(kr, hot), mid).astype(BF16)
        ww_ref[:, cols] = turned(dot(kw, hot), mid).astype(BF16)
        we_ref[:, cols] = turned(dot(ke, hot), s4).astype(BF16)

    lane = iota((1, 128), 1)
    copy_s.wait()
    rows = mid * ORIENT
    for tap in range(9):
        flat_s[pl.ds(tap * rows, rows), :mid] = ks_v[tap].astype(F32).reshape(rows, mid)
    piece = lambda tap, u: flat_s[pl.ds(tap * rows + u % ORIENT, mid, stride=ORIENT), :]
    low = jnp.broadcast_to(lane < mid, (mid, 128))
    half = jnp.broadcast_to(lane < 2 * mid, (mid, 128))
    pairs = {}
    for tap in range(9):
        for u in range(ORIENT):
            pairs[tap, u] = jnp.where(low, piece(tap, u), pltpu.roll(piece(back_tap(tap, 1), u - 1), mid, 1))
    for tap in range(9):
        for u in range(ORIENT):
            quad = jnp.where(half, pairs[tap, u], pltpu.roll(pairs[back_tap(tap, 2), (u - 2) % ORIENT], 2 * mid, 1)).astype(BF16)
            ws_ref[pl.ds(tap * rows + u * mid, mid), :128] = quad
            ahead = back_tap(tap, -4)
            ws_ref[pl.ds(ahead * rows + (u + 4) % ORIENT * mid, mid), 128:] = quad

    copy_t.wait()
    rows_t = s4 * ORIENT
    for tap in range(9):
        flat_t[pl.ds(tap * rows_t, rows_t), :s4] = kt_v[tap].astype(F32).reshape(rows_t, s4)
    piece_t = lambda tap, u: flat_t[pl.ds(tap * rows_t + u % ORIENT, s4, stride=ORIENT), :]
    low_t = jnp.broadcast_to(lane < s4, (s4, 128))
    for tap in range(9):
        for u in range(ORIENT):
            pair = jnp.where(low_t, piece_t(tap, u), pltpu.roll(piece_t(back_tap(tap, 1), u - 1), s4, 1))
            k2_ref[pl.ds(tap * rows_t + u * s4, s4), :] = pair.astype(BF16)


def block_kernel(x_ref, dn_ref, up_ref, wr_ref, ws_ref, ww_ref, we_ref, k2_ref,
                 br_ref, bs_ref, bw_ref, be_ref, bt_ref,
                 three_ref, four_ref,
                 xs, mids, threes, fours, evens, sem):
    place, count = lax.axis_index("rows"), lax.axis_size("rows")
    cols = dn_ref.shape[0] // 2
    own = x_ref.shape[0]
    wide, mid = x_ref.shape[1], wr_ref.shape[0]
    s4 = we_ref.shape[0]
    strips = own // cols
    copies = [
        pltpu.make_async_copy(dn_ref, xs.at[pl.ds(0, 2 * cols)], sem.at[0]),
        pltpu.make_async_copy(x_ref, xs.at[pl.ds(2 * cols, own)], sem.at[1]),
        pltpu.make_async_copy(up_ref, xs.at[pl.ds(2 * cols + own, cols)], sem.at[2]),
    ]
    for copy in copies:
        copy.start()
    tile = lambda fields, width: jnp.where(iota((fields, width), 1) % fields == iota((fields, width), 0), 1.0, 0.0).astype(BF16)
    b_red = bias_lanes(br_ref[...], tile(br_ref.shape[1], mid))
    b_mid = bias_lanes(bs_ref[...], tile(bs_ref.shape[1], mid))
    b_ent = bias_lanes(be_ref[...], tile(be_ref.shape[1], s4))
    b_str = bias_lanes(bt_ref[...], tile(bt_ref.shape[1], s4))
    b_wid = bias_lanes(bw_ref[...], spread(bw_ref.shape[1], 0, wide))
    not_first = jnp.where(place == 0, 0.0, 1.0)
    not_last = jnp.where(place == count - 1, 0.0, 1.0)
    for copy in copies:
        copy.wait()

    col = iota((cols, mid), 0)
    for row in range(strips + 3):
        y = dot_nt(xs[pl.ds(row * cols, cols), :], wr_ref[...]) + b_red
        y = jnp.maximum(y, 0.0)
        if row < 2:
            y = y * not_first
        if row == strips + 2:
            y = y * not_last
        at = pl.ds(row * cols, cols)
        mids[at, :mid] = jnp.where(col == 0, 0.0, pltpu.roll(y, 1, 0)).astype(BF16)
        mids[at, mid:2 * mid] = y.astype(BF16)
        mids[at, 2 * mid:] = jnp.where(col == cols - 1, 0.0, pltpu.roll(y, cols - 1, 0)).astype(BF16)

    for row in range(strips + 1):
        at = pl.ds(row * cols, cols)
        acc = b_mid
        for dy in range(3):
            acc = acc + dot(mids[pl.ds((row + dy) * cols, cols), :], ws_ref[pl.ds(dy * 3 * mid, 3 * mid), :])
        two = jnp.maximum(acc, 0.0).astype(BF16)
        for first in range(0, wide, 256):
            part = slice(first, first + 256)
            z = xs[pl.ds((row + 1) * cols, cols), part].astype(F32) + dot(two, ww_ref[:, part]) + b_wid[:, part]
            threes[at, part] = jnp.maximum(z, 0.0).astype(BF16)
        f = jnp.maximum(dot_nt(threes[at, :], we_ref[...]) + b_ent, 0.0)
        if row == 0:
            f = f * not_first
        for g in range(s4 // 128):
            fours[g, at, :] = f[:, g * 128:(g + 1) * 128]
    out = pltpu.make_async_copy(threes.at[pl.ds(cols, own)], three_ref, sem.at[3])
    out.start()

    half = cols // 2
    col = iota((half, 128), 0)
    for row in range(strips + 1):
        at = pl.ds(row * half, half)
        for g in range(s4 // 128):
            even = fours[g, pl.ds(row * cols, half, stride=2), :]
            odd = fours[g, pl.ds(row * cols + 1, half, stride=2), :]
            evens[at, pl.ds(g * 128, 128)] = jnp.where(col == 0, 0.0, pltpu.roll(odd, 1, 0)).astype(BF16)
            evens[at, pl.ds(s4 + g * 128, 128)] = even.astype(BF16)
            evens[at, pl.ds(2 * s4 + g * 128, 128)] = odd.astype(BF16)

    def filter_tile(tap, pair):
        halves = []
        for j in (2 * pair, 2 * pair + 1):
            source = back_tap(tap, 2 * j)
            halves.append(rows_rolled(k2_ref[pl.ds(source * s4, s4), :], 128 * j))
        return jnp.concatenate(halves, 1)

    results = []
    for pair in range(s4 // 256):
        acc = b_str[:, pair * 256:(pair + 1) * 256]
        for tap in range(9):
            dy, dx = divmod(tap, 3)
            lhs = jnp.concatenate(
                [evens[pl.ds((2 * q + dy) * half, half), dx * s4:(dx + 1) * s4] for q in range(strips // 2)], 0)
            acc = acc + dot(lhs, filter_tile(tap, pair))
        results.append(jnp.maximum(acc, 0.0).astype(BF16))
    result = jnp.concatenate(results, 1)
    fields = s4 // ORIENT
    a, b = iota((s4, s4), 0), iota((s4, s4), 1)
    order = jnp.where(b == (a % fields) * ORIENT + a // fields, 1.0, 0.0).astype(BF16)
    four_ref[...] = dot(result, order).astype(BF16)
    out.wait()


def shards(scene_map, reduce_kernel, reduce_bias, spatial_kernel, spatial_bias, widen_kernel, widen_bias,
           entry_kernel, entry_bias, stride_kernel, stride_bias):
    count = lax.axis_size("rows")
    down = lax.ppermute(scene_map[-2:], "rows", [(i, i + 1) for i in range(count - 1)])
    up = lax.ppermute(scene_map[:1], "rows", [(i + 1, i) for i in range(count - 1)])

    strips, cols, wide = scene_map.shape
    mid_f, s4_f = reduce_kernel.shape[2], entry_kernel.shape[2]
    mid, s4 = mid_f * ORIENT, s4_f * ORIENT
    any_spec = pl.BlockSpec(memory_space=pl.ANY)
    vmem = pl.BlockSpec(memory_space=pltpu.VMEM)
    dma = pltpu.SemaphoreType.DMA
    filters = pl.pallas_call(
        unfold_kernel,
        out_shape=[
            pltpu.VMEM((mid, wide), BF16),
            pltpu.VMEM((9 * mid, mid), BF16),
            pltpu.VMEM((mid, wide), BF16),
            pltpu.VMEM((s4, wide), BF16),
            pltpu.VMEM((9 * s4, 128), BF16),
        ],
        in_specs=[vmem, any_spec, vmem, vmem, any_spec],
        out_specs=[vmem] * 5,
        scratch_shapes=[
            pltpu.VMEM(spatial_kernel.shape, BF16),
            pltpu.VMEM(stride_kernel.shape, BF16),
            pltpu.VMEM((mid, wide // ORIENT), F32),
            pltpu.VMEM((9 * mid, 128), F32),
            pltpu.VMEM((9 * s4, 128), F32),
            dma((2,)),
        ],
        compiler_params=pltpu.CompilerParams(vmem_limit_bytes=24 << 20),
        name="unfold",
    )(reduce_kernel.transpose(1, 2, 0), spatial_kernel, widen_kernel, entry_kernel.transpose(1, 2, 0), stride_kernel)

    flat = lambda x: x.reshape(-1, wide)
    three, four = pl.pallas_call(
        block_kernel,
        out_shape=[
            jax.ShapeDtypeStruct((strips * cols, wide), BF16),
            jax.ShapeDtypeStruct((strips // 2 * (cols // 2), s4), BF16),
        ],
        in_specs=[any_spec] * 3 + [vmem] * 10,
        out_specs=[any_spec, vmem],
        scratch_shapes=[
            pltpu.VMEM(((strips + 3) * cols, wide), BF16),
            pltpu.VMEM(((strips + 3) * cols, 3 * mid), BF16),
            pltpu.VMEM(((strips + 1) * cols, wide), BF16),
            pltpu.VMEM((s4 // 128, (strips + 1) * cols, 128), F32),
            pltpu.VMEM(((strips + 1) * (cols // 2), 3 * s4), BF16),
            dma((4,)),
        ],
        compiler_params=pltpu.CompilerParams(vmem_limit_bytes=32 << 20),
        name="block",
    )(flat(scene_map), flat(down), flat(up), *filters,
      reduce_bias[None], spatial_bias[None], widen_bias[None], entry_bias[None], stride_bias[None])
    return three.reshape(strips, cols, wide), four.reshape(strips // 2, cols // 2, s4)


def solution(mesh):
    rows = P(("groups", "rows"), None, None)
    return jax.shard_map(shards, mesh=mesh, in_specs=(rows,) + (P(),) * 10, out_specs=(rows, rows), check_vma=False)
```

```python
import functools

import jax
import jax.numpy as jnp
from jax import lax
from jax.experimental import pallas as pl
from jax.experimental.pallas import tpu as pltpu
from jax.sharding import PartitionSpec as P

ORIENT = 8
CYCLE_TAPS = [0, 1, 2, 5, 8, 7, 6, 3]
BF16, F32 = jnp.bfloat16, jnp.float32
NT = (((1,), (1,)), ((), ()))


def back_tap(tap, turn):
    if tap == 4:
        return 4
    return CYCLE_TAPS[(CYCLE_TAPS.index(tap) - turn) % ORIENT]


def iota(shape, dim):
    return lax.broadcasted_iota(jnp.int32, shape, dim)


def dot(a, b):
    return jnp.dot(a, b, preferred_element_type=F32)


def dot_nt(a, b):
    return lax.dot_general(a, b, NT, preferred_element_type=F32)


def rows_rolled(x, by):
    by %= x.shape[0]
    if by == 0:
        return x
    return jnp.concatenate([x[x.shape[0] - by:], x[:x.shape[0] - by]], 0)


def spread(fields, first, width):
    return jnp.where((iota((fields, width), 1) + first) // ORIENT == iota((fields, width), 0), 1.0, 0.0).astype(BF16)


def turned(blocks, block):
    lane = iota((1, blocks.shape[1]), 1)
    for bit in (1, 2, 4):
        take = jnp.broadcast_to(lane & bit, blocks.shape) != 0
        blocks = jnp.where(take, rows_rolled(blocks, bit * block), blocks)
    return blocks


def bias_lanes(bias, hot):
    first = bias.astype(BF16)
    rest = bias - first.astype(F32)
    second = rest.astype(BF16)
    third = (rest - second.astype(F32)).astype(BF16)
    parts = [dot(jnp.broadcast_to(p, (16,) + p.shape[1:]), hot)[:1] for p in (first, second, third)]
    return parts[0] + parts[1] + parts[2]


def shifted(y, cols):
    col = iota(y.shape, 0)
    left = jnp.where(col == 0, 0.0, pltpu.roll(y, 1, 0))
    right = jnp.where(col == cols - 1, 0.0, pltpu.roll(y, cols - 1, 0))
    return jnp.concatenate([left, y, right], 1).astype(BF16)


def tile_hot(fields, width):
    return jnp.where(iota((fields, width), 1) % fields == iota((fields, width), 0), 1.0, 0.0).astype(BF16)


def fetched(pairs, sem, first=0):
    copies = [pltpu.make_async_copy(source, target, sem.at[first + n]) for n, (source, target) in enumerate(pairs)]
    for copy in copies:
        copy.start()
    return copies


def reduce_kernel_body(x_ref, kr_hbm, br_hbm, xs_ref, wr_ref, bias_ref, mids_ref, down_ref, up_ref, kr_ref, br_ref, sem):
    cols = up_ref.shape[0]
    strips = x_ref.shape[0] // cols
    small = fetched([(kr_hbm, kr_ref), (br_hbm, br_ref)], sem, strips)
    copies = []
    for row in range(strips):
        at = pl.ds(row * cols, cols)
        copies.append(pltpu.make_async_copy(x_ref.at[at], xs_ref.at[at], sem.at[row]))
        copies[-1].start()
    in_f, mid_f = kr_ref.shape[2], kr_ref.shape[1]
    wide, mid = in_f * ORIENT, mid_f * ORIENT
    for copy in small:
        copy.wait()
    kr = kr_ref[...].reshape(mid, in_f)
    kr = jnp.concatenate([kr[(-r) % ORIENT * mid_f:((-r) % ORIENT + 1) * mid_f] for r in range(ORIENT)], 0)
    for first in range(0, wide, 256):
        wr_ref[:, pl.ds(first, 256)] = turned(dot(kr, spread(in_f, first, 256)), mid_f).astype(BF16)
    bias = bias_lanes(br_ref[...], tile_hot(mid_f, mid))
    bias_ref[...] = bias
    for copy in copies:
        copy.wait()
    y = jnp.maximum(dot_nt(xs_ref[...], wr_ref[...]) + bias, 0.0)
    for row in range(strips):
        part = y[row * cols:(row + 1) * cols]
        mids_ref[pl.ds(row * cols, cols), :] = shifted(part, cols)
        if row == 0:
            up_ref[...] = part.astype(BF16)
        if row == strips - 2:
            down_ref[:, wide:] = part.astype(BF16)
    down_ref[:, :wide] = xs_ref[pl.ds((strips - 1) * cols, cols), :]


def strip_block(windows, x, ws_ref, ww_ref, we_ref, b_mid, b_wid, b_ent, threes):
    acc = b_mid
    depth = windows[0].shape[1]
    for dy in range(3):
        acc = acc + dot(windows[dy], ws_ref[pl.ds(dy * depth, depth), :])
    two = jnp.maximum(acc, 0.0).astype(BF16)
    for first in range(0, ww_ref.shape[1], 256):
        part = slice(first, first + 256)
        z = x(part).astype(F32) + dot(two, ww_ref[:, part]) + b_wid[:, part]
        threes[:, part] = jnp.maximum(z, 0.0).astype(BF16)
    return jnp.maximum(dot_nt(threes[...], we_ref[...]) + b_ent, 0.0)


def thirds(fours, f, strip, slot, cols, phases):
    half = cols // 2
    groups = f.shape[1] // 128
    for g in range(groups):
        fours[g, pl.ds(strip * cols, cols), :] = f[strip * cols:(strip + 1) * cols, g * 128:(g + 1) * 128]
    col = iota((half, 128), 0)
    for g in range(groups):
        even = fours[g, pl.ds(strip * cols, half, stride=2), :]
        odd = fours[g, pl.ds(strip * cols + 1, half, stride=2), :]
        moved = jnp.where(col == 0, 0.0, pltpu.roll(odd, 1, 0))
        for n, value in enumerate((moved, even, odd)):
            phases[pl.ds(slot * half, half), pl.ds((n * groups + g) * 128, 128)] = value.astype(BF16)


def inner_kernel(xs_ref, mids_ref, ks_hbm, kw_hbm, ke_hbm, kt_hbm, bs_hbm, bw_hbm, be_hbm, bt_hbm,
                 three_ref, ws_ref, ww_ref, we_ref, k2_ref, order_ref, b_mid_ref, b_wid_ref, b_ent_ref, b_str_ref, phases_ref,
                 ks_v, kw_ref, ke_ref, kt_v, bs_ref, bw_ref, be_ref, bt_ref, flat_w, flat_s, flat_t, threes, fours, sem):
    small = fetched([(ke_hbm, ke_ref), (kw_hbm, kw_ref), (bs_hbm, bs_ref), (bw_hbm, bw_ref), (be_hbm, be_ref), (bt_hbm, bt_ref)], sem, 1)
    large = fetched([(ks_hbm, ks_v), (kt_hbm, kt_v)], sem, 7)
    in_f, s4_f, mid_f = ke_ref.shape[2], ke_ref.shape[1], kw_ref.shape[0]
    wide, s4, mid = in_f * ORIENT, s4_f * ORIENT, mid_f * ORIENT
    cols = phases_ref.shape[0]
    strips = xs_ref.shape[0] // cols
    a, b = iota((s4, s4), 0), iota((s4, s4), 1)
    order_ref[...] = jnp.where(b == (a % s4_f) * ORIENT + a // s4_f, 1.0, 0.0).astype(BF16)
    for copy in small:
        copy.wait()
    ke = ke_ref[...].reshape(s4, in_f)
    ke = jnp.concatenate([ke[(-r) % ORIENT * s4_f:((-r) % ORIENT + 1) * s4_f] for r in range(ORIENT)], 0)
    flat_w[...] = kw_ref[...].astype(F32).reshape(mid, in_f)
    kw = jnp.concatenate([flat_w[pl.ds(u, mid_f, stride=ORIENT), :] for u in range(ORIENT)], 0).astype(BF16)
    for first in range(0, wide, 256):
        hot = spread(in_f, first, 256)
        cut = pl.ds(first, 256)
        ww_ref[:, cut] = turned(dot(kw, hot), mid_f).astype(BF16)
        we_ref[:, cut] = turned(dot(ke, hot), s4_f).astype(BF16)
    b_mid_ref[...] = bias_lanes(bs_ref[...], tile_hot(mid_f, mid))
    b_ent_ref[...] = bias_lanes(be_ref[...], tile_hot(s4_f, s4))
    b_str_ref[...] = bias_lanes(bt_ref[...], tile_hot(s4_f, s4))
    b_wid_ref[...] = bias_lanes(bw_ref[...], spread(in_f, 0, wide))

    lane = iota((1, 128), 1)
    large[0].wait()
    for tap in range(9):
        flat_s[pl.ds(tap * mid, mid), :mid_f] = ks_v[tap].astype(F32).reshape(mid, mid_f)
    piece = lambda tap, u: flat_s[pl.ds(tap * mid + u % ORIENT, mid_f, stride=ORIENT), :]
    low = jnp.broadcast_to(lane < mid_f, (mid_f, 128))
    half = jnp.broadcast_to(lane < 2 * mid_f, (mid_f, 128))
    pairs = {}
    for tap in range(9):
        for u in range(ORIENT):
            pairs[tap, u] = jnp.where(low, piece(tap, u), pltpu.roll(piece(back_tap(tap, 1), u - 1), mid_f, 1))
    for tap in range(9):
        for u in range(ORIENT):
            quad = jnp.where(half, pairs[tap, u], pltpu.roll(pairs[back_tap(tap, 2), (u - 2) % ORIENT], 2 * mid_f, 1)).astype(BF16)
            ws_ref[pl.ds(tap * mid + u * mid_f, mid_f), :128] = quad
            ahead = back_tap(tap, -4)
            ws_ref[pl.ds(ahead * mid + (u + 4) % ORIENT * mid_f, mid_f), 128:] = quad

    large[1].wait()
    for tap in range(9):
        flat_t[pl.ds(tap * s4, s4), :s4_f] = kt_v[tap].astype(F32).reshape(s4, s4_f)
    piece_t = lambda tap, u: flat_t[pl.ds(tap * s4 + u % ORIENT, s4_f, stride=ORIENT), :]
    low_t = jnp.broadcast_to(lane < s4_f, (s4_f, 128))
    for tap in range(9):
        for u in range(ORIENT):
            pair = jnp.where(low_t, piece_t(tap, u), pltpu.roll(piece_t(back_tap(tap, 1), u - 1), s4_f, 1))
            k2_ref[pl.ds(tap * s4 + u * s4_f, s4_f), :] = pair.astype(BF16)

    inner = strips - 2
    windows = [mids_ref[pl.ds(dy * cols, inner * cols), :] for dy in range(3)]
    f = strip_block(windows, lambda part: xs_ref[pl.ds(cols, inner * cols), part], ws_ref, ww_ref, we_ref,
                    b_mid_ref[...], b_wid_ref[...], b_ent_ref[...], threes)
    out = pltpu.make_async_copy(threes, three_ref.at[pl.ds(cols, inner * cols)], sem.at[0])
    out.start()
    for strip in range(inner):
        thirds(fours, f, strip, strip, cols, phases_ref)
    out.wait()


def edge_kernel(down_ref, up_ref, xs_ref, wr_ref, bias_ref, mids_ref, ws_ref, ww_ref, we_ref, k2_ref, order_ref,
                b_mid_ref, b_wid_ref, b_ent_ref, b_str_ref, inner_ref, kept_ref,
                three_ref, four_ref, xe, threes, fours, phases, sem):
    place, count = lax.axis_index("rows"), lax.axis_size("rows")
    cols = up_ref.shape[0]
    half = cols // 2
    strips = xs_ref.shape[0] // cols
    wide, mid, s4 = xs_ref.shape[1], wr_ref.shape[0], we_ref.shape[0]
    not_first = jnp.where(place == 0, 0.0, 1.0)
    not_last = jnp.where(place == count - 1, 0.0, 1.0)
    strip_of = lambda row: mids_ref[pl.ds(row * cols, cols), :]
    xe[pl.ds(0, cols), :] = down_ref[:, :wide]
    xe[pl.ds(cols, cols), :] = xs_ref[pl.ds(0, cols), :]
    xe[pl.ds(2 * cols, cols), :] = xs_ref[pl.ds((strips - 1) * cols, cols), :]
    above_two = shifted(down_ref[:, wide:].astype(F32) * not_first, cols)
    y = jnp.maximum(dot_nt(down_ref[:, :wide], wr_ref[...]) + bias_ref[...], 0.0) * not_first
    above = shifted(y, cols)
    below = shifted(up_ref[...].astype(F32) * not_last, cols)
    last = strips - 1
    windows = [
        jnp.concatenate([above_two, above, strip_of(last - 1)], 0),
        jnp.concatenate([above, strip_of(0), strip_of(last)], 0),
        jnp.concatenate([strip_of(0), strip_of(1), below], 0),
    ]
    f = strip_block(windows, lambda part: xe[:, part], ws_ref, ww_ref, we_ref,
                    b_mid_ref[...], b_wid_ref[...], b_ent_ref[...], threes)
    outs = [
        pltpu.make_async_copy(threes.at[pl.ds(cols, cols)], three_ref.at[pl.ds(0, cols)], sem.at[0]),
        pltpu.make_async_copy(threes.at[pl.ds(2 * cols, cols)], three_ref.at[pl.ds(last * cols, cols)], sem.at[1]),
    ]
    for out in outs:
        out.start()
    f = jnp.concatenate([f[:cols] * not_first, f[cols:]], 0)
    for strip in range(3):
        thirds(fours, f, strip, strip, cols, phases)

    def rows_of(row, dx):
        cut = slice(dx * s4, (dx + 1) * s4)
        if row < 1:
            return phases[pl.ds((row + 1) * half, half), cut]
        if row == last:
            return phases[pl.ds(2 * half, half), cut]
        return inner_ref[pl.ds((row - 1) * half, half), cut]

    def filter_tile(tap, pair):
        halves = []
        for j in (2 * pair, 2 * pair + 1):
            source = back_tap(tap, 2 * j)
            halves.append(rows_rolled(k2_ref[pl.ds(source * s4, s4), :], 128 * j))
        return jnp.concatenate(halves, 1)

    lhs = []
    for tap in range(9):
        dy, dx = divmod(tap, 3)
        lhs.append(jnp.concatenate([rows_of(2 * q + dy - 1, dx) for q in range(strips // 2)], 0))
    results = []
    for pair in range(s4 // 256):
        acc = b_str_ref[:, pair * 256:(pair + 1) * 256]
        for tap in range(9):
            acc = acc + dot(lhs[tap], filter_tile(tap, pair))
        results.append(jnp.maximum(acc, 0.0).astype(BF16))
    four_ref[...] = dot(jnp.concatenate(results, 1), order_ref[...]).astype(BF16)
    for out in outs:
        out.wait()


def shards(scene_map, reduce_kernel, reduce_bias, spatial_kernel, spatial_bias, widen_kernel, widen_bias,
           entry_kernel, entry_bias, stride_kernel, stride_bias):
    count = lax.axis_size("rows")
    strips, cols, wide = scene_map.shape
    mid_f, s4_f = reduce_kernel.shape[2], entry_kernel.shape[2]
    mid, s4 = mid_f * ORIENT, s4_f * ORIENT
    own, half = strips * cols, cols // 2
    hbm = pl.BlockSpec(memory_space=pl.ANY)
    vmem = pl.BlockSpec(memory_space=pltpu.VMEM)
    dma = pltpu.SemaphoreType.DMA
    limit = lambda mib: pltpu.CompilerParams(vmem_limit_bytes=mib << 20)

    pinned = lambda *arrays: [pltpu.with_memory_space_constraint(a, pltpu.HBM) for a in arrays]
    xs, w_reduce, b_reduce, mids, down, up = pl.pallas_call(
        reduce_kernel_body,
        out_shape=[
            pltpu.VMEM((own, wide), BF16),
            pltpu.VMEM((mid, wide), BF16),
            pltpu.VMEM((1, mid), F32),
            pltpu.VMEM((own, 3 * mid), BF16),
            pltpu.VMEM((cols, wide + mid), BF16),
            pltpu.VMEM((cols, mid), BF16),
        ],
        in_specs=[hbm] * 3,
        out_specs=[vmem] * 6,
        scratch_shapes=[
            pltpu.VMEM((ORIENT, mid_f, wide // ORIENT), BF16),
            pltpu.VMEM((1, mid_f), F32),
            dma((strips + 2,)),
        ],
        compiler_params=limit(16),
        name="reduce",
    )(*pinned(scene_map.reshape(own, wide), reduce_kernel.transpose(1, 2, 0), reduce_bias[None]))
    down = lax.ppermute(down, "rows", [(i, i + 1) for i in range(count - 1)])
    up = lax.ppermute(up, "rows", [(i + 1, i) for i in range(count - 1)])

    three, *kept, phases = pl.pallas_call(
        inner_kernel,
        out_shape=[
            jax.ShapeDtypeStruct((own, wide), BF16),
            pltpu.VMEM((9 * mid, mid), BF16),
            pltpu.VMEM((mid, wide), BF16),
            pltpu.VMEM((s4, wide), BF16),
            pltpu.VMEM((9 * s4, 128), BF16),
            pltpu.VMEM((s4, s4), BF16),
            pltpu.VMEM((1, mid), F32),
            pltpu.VMEM((1, wide), F32),
            pltpu.VMEM((1, s4), F32),
            pltpu.VMEM((1, s4), F32),
            pltpu.VMEM(((strips - 2) * half, 3 * s4), BF16),
        ],
        in_specs=[vmem] * 2 + [hbm] * 8,
        out_specs=[hbm] + [vmem] * 10,
        scratch_shapes=[
            pltpu.VMEM(spatial_kernel.shape, BF16),
            pltpu.VMEM(widen_kernel.shape, BF16),
            pltpu.VMEM((ORIENT, s4_f, wide // ORIENT), BF16),
            pltpu.VMEM(stride_kernel.shape, BF16),
            pltpu.VMEM((1, mid_f), F32),
            pltpu.VMEM((1, wide // ORIENT), F32),
            pltpu.VMEM((1, s4_f), F32),
            pltpu.VMEM((1, s4_f), F32),
            pltpu.VMEM((mid, wide // ORIENT), F32),
            pltpu.VMEM((9 * mid, 128), F32),
            pltpu.VMEM((9 * s4, 128), F32),
            pltpu.VMEM(((strips - 2) * cols, wide), BF16),
            pltpu.VMEM((s4 // 128, (strips - 2) * cols, 128), F32),
            dma((9,)),
        ],
        compiler_params=limit(28),
        name="inner",
    )(xs, mids, *pinned(spatial_kernel, widen_kernel, entry_kernel.transpose(1, 2, 0), stride_kernel,
                         spatial_bias[None], widen_bias[None], entry_bias[None], stride_bias[None]))

    operands = [down, up, xs, w_reduce, b_reduce, mids, *kept, phases, three]
    three, four = pl.pallas_call(
        edge_kernel,
        out_shape=[
            jax.ShapeDtypeStruct((own, wide), BF16),
            jax.ShapeDtypeStruct((strips // 2 * half, s4), BF16),
        ],
        in_specs=[vmem] * (len(operands) - 1) + [hbm],
        out_specs=[hbm, vmem],
        input_output_aliases={len(operands) - 1: 0},
        scratch_shapes=[
            pltpu.VMEM((3 * cols, wide), BF16),
            pltpu.VMEM((3 * cols, wide), BF16),
            pltpu.VMEM((s4 // 128, 3 * cols, 128), F32),
            pltpu.VMEM((3 * half, 3 * s4), BF16),
            dma((2,)),
        ],
        compiler_params=limit(28),
        name="edge",
    )(*operands)
    return three.reshape(strips, cols, wide), four.reshape(strips // 2, half, s4)


def solution(mesh):
    rows = P(("groups", "rows"), None, None)
    return jax.shard_map(shards, mesh=mesh, in_specs=(rows,) + (P(),) * 10, out_specs=(rows, rows), check_vma=False)
```

```python
import functools

import jax
import jax.numpy as jnp
from jax import lax
from jax.experimental import pallas as pl
from jax.experimental.pallas import tpu as pltpu
from jax.sharding import PartitionSpec as P

ORIENT = 8
BLOCK = 128
CYCLE_TAPS = [0, 1, 2, 5, 8, 7, 6, 3]
BF16, F32 = jnp.bfloat16, jnp.float32
NT = (((1,), (1,)), ((), ()))


def back_tap(tap, turn):
    if tap == 4:
        return 4
    return CYCLE_TAPS[(CYCLE_TAPS.index(tap) - turn) % ORIENT]


def iota(shape, dim):
    return lax.broadcasted_iota(jnp.int32, shape, dim)


def dot(a, b):
    return jnp.dot(a, b, preferred_element_type=F32)


def dot_nt(a, b):
    return lax.dot_general(a, b, NT, preferred_element_type=F32)


def rows_rolled(x, by):
    by %= x.shape[0]
    if by == 0:
        return x
    return jnp.concatenate([x[x.shape[0] - by:], x[:x.shape[0] - by]], 0)


def spread(fields, first, width):
    lead = iota((fields, width), 1) + first - ORIENT * iota((fields, width), 0)
    return jnp.where(lead & -ORIENT == 0, 1.0, 0.0).astype(BF16)


def turned(blocks, block):
    lane = iota((1, blocks.shape[1]), 1)
    for bit in (1, 2, 4):
        take = jnp.broadcast_to(lane & bit, blocks.shape) != 0
        blocks = jnp.where(take, rows_rolled(blocks, bit * block), blocks)
    return blocks


def unfold_in(kernel, fields, store):
    inputs = kernel.shape[1]
    base = jnp.concatenate([kernel[(-r) % ORIENT * fields:((-r) % ORIENT + 1) * fields] for r in range(ORIENT)], 0)
    base, other = base.T, rows_rolled(base, fields).T
    for first in range(0, inputs * ORIENT, 128):
        lead = iota((128, inputs), 0) + first - ORIENT * iota((128, inputs), 1)
        hot = jnp.where(lead & -ORIENT == 0, 1.0, 0.0).astype(BF16)
        row = iota((128, fields * ORIENT), 0)
        block = jnp.where(row & 1 != 0, dot(hot, other), dot(hot, base))
        for bit in (2, 4):
            block = jnp.where(row & bit != 0, pltpu.roll(block, bit * fields, 1), block)
        store(pl.ds(first, 128), block.astype(BF16))


def bias_lanes(bias, hot):
    first = bias.astype(BF16)
    rest = bias - first.astype(F32)
    second = rest.astype(BF16)
    third = (rest - second.astype(F32)).astype(BF16)
    parts = [dot(jnp.broadcast_to(p, (16,) + p.shape[1:]), hot)[:1] for p in (first, second, third)]
    return parts[0] + parts[1] + parts[2]


def fetched(pairs, sem, first=0):
    copies = [pltpu.make_async_copy(source, target, sem.at[first + n]) for n, (source, target) in enumerate(pairs)]
    for copy in copies:
        copy.start()
    return copies


def shifted(y, cols):
    col = iota(y.shape, 0)
    left = jnp.where(col == 0, 0.0, pltpu.roll(y, 1, 0))
    right = jnp.where(col == cols - 1, 0.0, pltpu.roll(y, cols - 1, 0))
    return jnp.concatenate([left, y, right], 1).astype(BF16)


def tile_hot(fields, width):
    return jnp.where((iota((fields, width), 1) - iota((fields, width), 0)) & (fields - 1) == 0, 1.0, 0.0).astype(BF16)


def fetched(pairs, sem, first=0):
    copies = [pltpu.make_async_copy(source, target, sem.at[first + n]) for n, (source, target) in enumerate(pairs)]
    for copy in copies:
        copy.start()
    return copies


def load_kernel(x_hbm, kr_hbm, br_hbm, bs_hbm, bw_hbm, be_hbm, bt_hbm,
                xs_ref, last_ref, wr_ref, b_red_ref, b_mid_ref, b_wid_ref, b_ent_ref, b_str_ref, order_ref,
                kr_ref, br_ref, bs_ref, bw_ref, be_ref, bt_ref, sem):
    cols = last_ref.shape[0]
    own = x_hbm.shape[0]
    small = fetched([(kr_hbm, kr_ref), (br_hbm, br_ref), (bs_hbm, bs_ref), (bw_hbm, bw_ref), (be_hbm, be_ref), (bt_hbm, bt_ref)], sem)
    large = fetched([(x_hbm.at[pl.ds(own - cols, cols)], last_ref), (x_hbm, xs_ref)], sem, 6)
    in_f, mid_f, s4_f = kr_ref.shape[2], kr_ref.shape[1], be_ref.shape[1]
    wide, mid, s4 = in_f * ORIENT, mid_f * ORIENT, s4_f * ORIENT
    shift = s4_f.bit_length() - 1
    a, b = iota((s4, s4), 0), iota((s4, s4), 1)
    order_ref[...] = jnp.where(b == (a & (s4_f - 1)) * ORIENT + (a >> shift), 1.0, 0.0).astype(BF16)
    for copy in small:
        copy.wait()
    def keep(at, block):
        wr_ref[at, :] = block
    unfold_in(kr_ref[...].reshape(mid, in_f), mid_f, keep)
    hot_mid, hot_s4 = tile_hot(mid_f, mid), tile_hot(s4_f, s4)
    b_red_ref[...] = bias_lanes(br_ref[...], hot_mid)
    b_mid_ref[...] = bias_lanes(bs_ref[...], hot_mid)
    b_ent_ref[...] = bias_lanes(be_ref[...], hot_s4)
    b_str_ref[...] = bias_lanes(bt_ref[...], hot_s4)
    b_wid_ref[...] = bias_lanes(bw_ref[...], spread(in_f, 0, wide))
    for copy in large:
        copy.wait()


def reducing(xs_ref, wr_ref, bias_ref, mids_ref, first_ref, second_ref):
    cols = first_ref.shape[0]
    strips = xs_ref.shape[0] // cols
    even = lax.axis_index("groups") % 2 == 0
    y = jnp.maximum(dot(xs_ref[...], wr_ref[...]) + bias_ref[...], 0.0)
    parts = [y[row * cols:(row + 1) * cols] for row in range(strips)]
    first_ref[...] = jnp.where(even, parts[strips - 2], parts[0]).astype(BF16)
    second_ref[...] = jnp.where(even, parts[0], parts[strips - 2]).astype(BF16)
    for row, part in enumerate(parts):
        mids_ref[pl.ds(row * cols, cols), :] = shifted(part, cols)


def strip_block(windows, x, ws_ref, ww_ref, b_mid, b_wid, threes):
    depth = windows[0].shape[1]
    twos = []
    for m in range(0, threes.shape[0], BLOCK):
        acc = b_mid
        for dy in range(3):
            acc = acc + dot(windows[dy][m:m + BLOCK], ws_ref[pl.ds(dy * depth, depth), :])
        twos.append(jnp.maximum(acc, 0.0).astype(BF16))
    for m, two in enumerate(twos):
        at = pl.ds(m * BLOCK, BLOCK)
        for first in range(0, ww_ref.shape[1], 256):
            part = slice(first, first + 256)
            z = x(at, part).astype(F32) + dot(two, ww_ref[:, part]) + b_wid[:, part]
            threes[at, part] = jnp.maximum(z, 0.0).astype(BF16)


def entry_part(threes, we_ref, b_ent, row, first):
    cut = slice(first, first + 256)
    return jnp.maximum(dot(threes[pl.ds(row, BLOCK), :], we_ref[:, cut]) + b_ent[:, cut], 0.0)


def thirds(fours, threes, we_ref, b_ent, scale, strip, slot, cols, phases):
    half = cols // 2
    s4 = we_ref.shape[1]
    for first in range(0, s4, 256):
        f = entry_part(threes, we_ref, b_ent, strip * cols, first)
        if scale is not None:
            f = f * scale
        for g in range(2):
            fours[first // 128 + g, pl.ds(strip * cols, cols), :] = f[:, g * 128:(g + 1) * 128]
    col = iota((half, 128), 0)
    for g in range(s4 // 128):
        even = fours[g, pl.ds(strip * cols, half, stride=2), :]
        odd = fours[g, pl.ds(strip * cols + 1, half, stride=2), :]
        moved = jnp.where(col == 0, 0.0, pltpu.roll(odd, 1, 0))
        for n, value in enumerate((moved, even, odd)):
            phases[pl.ds(slot * half, half), pl.ds(n * s4 + g * 128, 128)] = value.astype(BF16)


def inner_kernel(xs_ref, mids_ref, b_mid_ref, b_wid_ref, b_ent_ref, ks_hbm, kw_hbm, ke_hbm, kt_hbm,
                 three_ref, ws_ref, ww_ref, we_ref, k2_ref, phases_ref,
                 ks_v, kw_ref, ke_ref, kt_v, flat_w, flat_s, flat_t, threes, fours, sem):
    copies = fetched([(kw_hbm, kw_ref), (ke_hbm, ke_ref), (ks_hbm, ks_v), (kt_hbm, kt_v)], sem, 1)
    in_f, s4_f, mid_f = ke_ref.shape[2], ke_ref.shape[1], kw_ref.shape[0]
    wide, s4, mid = in_f * ORIENT, s4_f * ORIENT, mid_f * ORIENT
    cols = phases_ref.shape[0]
    strips = xs_ref.shape[0] // cols
    copies[0].wait()
    flat_w[...] = kw_ref[...].astype(F32).reshape(mid, in_f)
    kw = jnp.concatenate([flat_w[pl.ds(u, mid_f, stride=ORIENT), :] for u in range(ORIENT)], 0).astype(BF16)
    for first in range(0, wide, 256):
        ww_ref[:, pl.ds(first, 256)] = turned(dot(kw, spread(in_f, first, 256)), mid_f).astype(BF16)
    copies[1].wait()
    def keep(at, block):
        we_ref[at, :] = block
    unfold_in(ke_ref[...].reshape(s4, in_f), s4_f, keep)

    lane = iota((1, 128), 1)
    copies[2].wait()
    for tap in range(9):
        flat_s[pl.ds(tap * mid, mid), :mid_f] = ks_v[tap].astype(F32).reshape(mid, mid_f)
    piece = lambda tap, u: flat_s[pl.ds(tap * mid + u % ORIENT, mid_f, stride=ORIENT), :]
    low = jnp.broadcast_to(lane < mid_f, (mid_f, 128))
    half = jnp.broadcast_to(lane < 2 * mid_f, (mid_f, 128))
    pairs = {}
    for tap in range(9):
        for u in range(ORIENT):
            pairs[tap, u] = jnp.where(low, piece(tap, u), pltpu.roll(piece(back_tap(tap, 1), u - 1), mid_f, 1))
    for tap in range(9):
        for u in range(ORIENT):
            quad = jnp.where(half, pairs[tap, u], pltpu.roll(pairs[back_tap(tap, 2), (u - 2) % ORIENT], 2 * mid_f, 1)).astype(BF16)
            ws_ref[pl.ds(tap * mid + u * mid_f, mid_f), :128] = quad
            ahead = back_tap(tap, -4)
            ws_ref[pl.ds(ahead * mid + (u + 4) % ORIENT * mid_f, mid_f), 128:] = quad

    copies[3].wait()
    for tap in range(9):
        flat_t[pl.ds(tap * s4, s4), :s4_f] = kt_v[tap].astype(F32).reshape(s4, s4_f)
    piece_t = lambda tap, u: flat_t[pl.ds(tap * s4 + u % ORIENT, s4_f, stride=ORIENT), :]
    low_t = jnp.broadcast_to(lane < s4_f, (s4_f, 128))
    for tap in range(9):
        for u in range(ORIENT):
            pair = jnp.where(low_t, piece_t(tap, u), pltpu.roll(piece_t(back_tap(tap, 1), u - 1), s4_f, 1))
            k2_ref[pl.ds(tap * s4 + u * s4_f, s4_f), :] = pair.astype(BF16)

    inner = strips - 2
    windows = [mids_ref[pl.ds(dy * cols, inner * cols), :] for dy in range(3)]
    strip_block(windows, lambda at, part: xs_ref[pl.ds(cols + at.start, at.size), part], ws_ref, ww_ref,
                b_mid_ref[...], b_wid_ref[...], threes)
    out = pltpu.make_async_copy(threes, three_ref.at[pl.ds(cols, inner * cols)], sem.at[0])
    out.start()
    for strip in range(inner):
        thirds(fours, threes, we_ref, b_ent_ref[...], None, strip, strip, cols, phases_ref)
    out.wait()


def edge_kernel(last_ref, first_ref, second_ref, xs_ref, wr_ref, bias_ref, b_mid_ref, b_wid_ref, b_ent_ref, b_str_ref, order_ref,
                mids_ref, ws_ref, ww_ref, we_ref, k2_ref, inner_ref, kept_ref,
                three_ref, four_ref, xe, threes, fours, phases, sem):
    place, count = lax.axis_index("rows"), lax.axis_size("rows")
    even = lax.axis_index("groups") % 2 == 0
    cols = first_ref.shape[0]
    half = cols // 2
    strips = xs_ref.shape[0] // cols
    wide, mid, s4 = xs_ref.shape[1], wr_ref.shape[1], we_ref.shape[1]
    not_first = jnp.where(place == 0, 0.0, 1.0)
    not_last = jnp.where(place == count - 1, 0.0, 1.0)
    strip_of = lambda row: mids_ref[pl.ds(row * cols, cols), :]
    xe[pl.ds(0, cols), :] = last_ref[...]
    xe[pl.ds(cols, cols), :] = xs_ref[pl.ds(0, cols), :]
    xe[pl.ds(2 * cols, cols), :] = xs_ref[pl.ds((strips - 1) * cols, cols), :]
    got = [first_ref[...].astype(F32), second_ref[...].astype(F32)]
    above_two = shifted(jnp.where(even, got[0], got[1]) * not_first, cols)
    y = jnp.maximum(dot(last_ref[...], wr_ref[...]) + bias_ref[...], 0.0) * not_first
    above = shifted(y, cols)
    below = shifted(jnp.where(even, got[1], got[0]) * not_last, cols)
    last = strips - 1
    windows = [
        jnp.concatenate([above_two, above, strip_of(last - 1)], 0),
        jnp.concatenate([above, strip_of(0), strip_of(last)], 0),
        jnp.concatenate([strip_of(0), strip_of(1), below], 0),
    ]
    strip_block(windows, lambda at, part: xe[at, part], ws_ref, ww_ref, b_mid_ref[...], b_wid_ref[...], threes)
    outs = [
        pltpu.make_async_copy(threes.at[pl.ds(cols, cols)], three_ref.at[pl.ds(0, cols)], sem.at[0]),
        pltpu.make_async_copy(threes.at[pl.ds(2 * cols, cols)], three_ref.at[pl.ds(last * cols, cols)], sem.at[1]),
    ]
    for out in outs:
        out.start()
    for strip in range(3):
        thirds(fours, threes, we_ref, b_ent_ref[...], None if strip else not_first, strip, strip, cols, phases)

    def rows_of(row, dx):
        cut = slice(dx * s4, (dx + 1) * s4)
        if row < 1:
            return phases[pl.ds((row + 1) * half, half), cut]
        if row == last:
            return phases[pl.ds(2 * half, half), cut]
        return inner_ref[pl.ds((row - 1) * half, half), cut]

    def filter_tile(tap, pair):
        halves = []
        for j in (2 * pair, 2 * pair + 1):
            source = back_tap(tap, 2 * j)
            halves.append(rows_rolled(k2_ref[pl.ds(source * s4, s4), :], 128 * j))
        return jnp.concatenate(halves, 1)

    lhs = []
    for tap in range(9):
        dy, dx = divmod(tap, 3)
        lhs.append(jnp.concatenate([rows_of(2 * q + dy - 1, dx) for q in range(strips // 2)], 0))
    results = []
    for pair in range(s4 // 256):
        acc = b_str_ref[:, pair * 256:(pair + 1) * 256]
        for tap in range(9):
            acc = acc + dot(lhs[tap], filter_tile(tap, pair))
        results.append(jnp.maximum(acc, 0.0).astype(BF16))
    four_ref[...] = dot(jnp.concatenate(results, 1), order_ref[...]).astype(BF16)
    for out in outs:
        out.wait()


def loops(groups, count):
    at = lambda group, row: group * count + row
    pairs = []
    for group in range(groups):
        step = 1 if group % 2 == 0 else -1
        for row in range(count):
            if 0 <= row + step < count:
                pairs.append((at(group, row), at(group, row + step)))
            elif group ^ 1 < groups:
                pairs.append((at(group, row), at(group ^ 1, row)))
    return pairs, [(b, a) for a, b in pairs]


def shards(scene_map, reduce_kernel, reduce_bias, spatial_kernel, spatial_bias, widen_kernel, widen_bias,
           entry_kernel, entry_bias, stride_kernel, stride_bias):
    count = lax.axis_size("rows")
    strips, cols, wide = scene_map.shape
    mid_f, s4_f = reduce_kernel.shape[2], entry_kernel.shape[2]
    mid, s4 = mid_f * ORIENT, s4_f * ORIENT
    own, half = strips * cols, cols // 2
    hbm = pl.BlockSpec(memory_space=pl.ANY)
    vmem = pl.BlockSpec(memory_space=pltpu.VMEM)
    dma = pltpu.SemaphoreType.DMA
    limit = lambda mib: pltpu.CompilerParams(vmem_limit_bytes=mib << 20)

    pinned = lambda *arrays: [pltpu.with_memory_space_constraint(a, pltpu.HBM) for a in arrays]
    xs, last, *known = pl.pallas_call(
        load_kernel,
        out_shape=[
            pltpu.VMEM((own, wide), BF16),
            pltpu.VMEM((cols, wide), BF16),
            pltpu.VMEM((wide, mid), BF16),
            pltpu.VMEM((1, mid), F32),
            pltpu.VMEM((1, mid), F32),
            pltpu.VMEM((1, wide), F32),
            pltpu.VMEM((1, s4), F32),
            pltpu.VMEM((1, s4), F32),
            pltpu.VMEM((s4, s4), BF16),
        ],
        in_specs=[hbm] * 7,
        out_specs=[vmem] * 9,
        scratch_shapes=[
            pltpu.VMEM((ORIENT, mid_f, wide // ORIENT), BF16),
            pltpu.VMEM((1, mid_f), F32),
            pltpu.VMEM((1, mid_f), F32),
            pltpu.VMEM((1, wide // ORIENT), F32),
            pltpu.VMEM((1, s4_f), F32),
            pltpu.VMEM((1, s4_f), F32),
            dma((8,)),
        ],
        compiler_params=limit(16),
        name="load",
    )(*pinned(scene_map.reshape(own, wide), reduce_kernel.transpose(1, 2, 0), reduce_bias[None],
              spatial_bias[None], widen_bias[None], entry_bias[None], stride_bias[None]))
    w_reduce, b_reduce, b_mid, b_wid, b_ent = known[:5]
    last = lax.ppermute(last, "rows", [(i, (i + 1) % count) for i in range(count)])
    mids, first, second = pl.pallas_call(
        reducing,
        out_shape=[
            pltpu.VMEM((own, 3 * mid), BF16),
            pltpu.VMEM((cols, mid), BF16),
            pltpu.VMEM((cols, mid), BF16),
        ],
        in_specs=[vmem] * 3,
        out_specs=[vmem] * 3,
        compiler_params=limit(16),
        name="reduce",
    )(xs, w_reduce, b_reduce)
    there, back = loops(lax.axis_size("groups"), count)
    first = lax.ppermute(first, ("groups", "rows"), there)
    second = lax.ppermute(second, ("groups", "rows"), back)

    three, *kept, phases = pl.pallas_call(
        inner_kernel,
        out_shape=[
            jax.ShapeDtypeStruct((own, wide), BF16),
            pltpu.VMEM((9 * mid, mid), BF16),
            pltpu.VMEM((mid, wide), BF16),
            pltpu.VMEM((wide, s4), BF16),
            pltpu.VMEM((9 * s4, 128), BF16),
            pltpu.VMEM(((strips - 2) * half, 3 * s4), BF16),
        ],
        in_specs=[vmem] * 5 + [hbm] * 4,
        out_specs=[hbm] + [vmem] * 5,
        scratch_shapes=[
            pltpu.VMEM(spatial_kernel.shape, BF16),
            pltpu.VMEM(widen_kernel.shape, BF16),
            pltpu.VMEM((ORIENT, s4_f, wide // ORIENT), BF16),
            pltpu.VMEM(stride_kernel.shape, BF16),
            pltpu.VMEM((mid, wide // ORIENT), F32),
            pltpu.VMEM((9 * mid, 128), F32),
            pltpu.VMEM((9 * s4, 128), F32),
            pltpu.VMEM(((strips - 2) * cols, wide), BF16),
            pltpu.VMEM((s4 // 128, (strips - 2) * cols, 128), F32),
            dma((5,)),
        ],
        compiler_params=limit(28),
        name="inner",
    )(xs, mids, b_mid, b_wid, b_ent, *pinned(spatial_kernel, widen_kernel, entry_kernel.transpose(1, 2, 0), stride_kernel))

    operands = [last, first, second, xs, *known, mids, *kept, phases, three]
    three, four = pl.pallas_call(
        edge_kernel,
        out_shape=[
            jax.ShapeDtypeStruct((own, wide), BF16),
            jax.ShapeDtypeStruct((strips // 2 * half, s4), BF16),
        ],
        in_specs=[vmem] * (len(operands) - 1) + [hbm],
        out_specs=[hbm, vmem],
        input_output_aliases={len(operands) - 1: 0},
        scratch_shapes=[
            pltpu.VMEM((3 * cols, wide), BF16),
            pltpu.VMEM((3 * cols, wide), BF16),
            pltpu.VMEM((s4 // 128, 3 * cols, 128), F32),
            pltpu.VMEM((3 * half, 3 * s4), BF16),
            dma((2,)),
        ],
        compiler_params=limit(28),
        name="edge",
    )(*operands)
    return three.reshape(strips, cols, wide), four.reshape(strips // 2, half, s4)


def solution(mesh):
    rows = P(("groups", "rows"), None, None)
    return jax.shard_map(shards, mesh=mesh, in_specs=(rows,) + (P(),) * 10, out_specs=(rows, rows), check_vma=False)
```

```python
import functools

import jax
import jax.numpy as jnp
from jax import lax
from jax.experimental import pallas as pl
from jax.experimental.pallas import tpu as pltpu
from jax.sharding import PartitionSpec as P

ORIENT = 8
BLOCK = 128
CYCLE_TAPS = [0, 1, 2, 5, 8, 7, 6, 3]
BF16, F32 = jnp.bfloat16, jnp.float32
NT = (((1,), (1,)), ((), ()))


def back_tap(tap, turn):
    if tap == 4:
        return 4
    return CYCLE_TAPS[(CYCLE_TAPS.index(tap) - turn) % ORIENT]


def iota(shape, dim):
    return lax.broadcasted_iota(jnp.int32, shape, dim)


def dot(a, b):
    return jnp.dot(a, b, preferred_element_type=F32)


def dot_nt(a, b):
    return lax.dot_general(a, b, NT, preferred_element_type=F32)


def rows_rolled(x, by):
    by %= x.shape[0]
    if by == 0:
        return x
    return jnp.concatenate([x[x.shape[0] - by:], x[:x.shape[0] - by]], 0)


def spread(fields, first, width):
    lead = iota((fields, width), 1) + first - ORIENT * iota((fields, width), 0)
    return jnp.where(lead & -ORIENT == 0, 1.0, 0.0).astype(BF16)


def turned(blocks, block):
    lane = iota((1, blocks.shape[1]), 1)
    for bit in (1, 2, 4):
        take = jnp.broadcast_to(lane & bit, blocks.shape) != 0
        blocks = jnp.where(take, rows_rolled(blocks, bit * block), blocks)
    return blocks


def unfold_in(kernel, fields, store):
    inputs = kernel.shape[1]
    base = jnp.concatenate([kernel[(-r) % ORIENT * fields:((-r) % ORIENT + 1) * fields] for r in range(ORIENT)], 0)
    base, other = base.T, rows_rolled(base, fields).T
    for first in range(0, inputs * ORIENT, 128):
        lead = iota((128, inputs), 0) + first - ORIENT * iota((128, inputs), 1)
        hot = jnp.where(lead & -ORIENT == 0, 1.0, 0.0).astype(BF16)
        row = iota((128, fields * ORIENT), 0)
        block = jnp.where(row & 1 != 0, dot(hot, other), dot(hot, base))
        for bit in (2, 4):
            block = jnp.where(row & bit != 0, pltpu.roll(block, bit * fields, 1), block)
        store(pl.ds(first, 128), block.astype(BF16))


def bias_lanes(bias, hot):
    first = bias.astype(BF16)
    rest = bias - first.astype(F32)
    second = rest.astype(BF16)
    third = (rest - second.astype(F32)).astype(BF16)
    parts = [dot(jnp.broadcast_to(p, (16,) + p.shape[1:]), hot)[:1] for p in (first, second, third)]
    return parts[0] + parts[1] + parts[2]


def fetched(pairs, sem, first=0):
    copies = [pltpu.make_async_copy(source, target, sem.at[first + n]) for n, (source, target) in enumerate(pairs)]
    for copy in copies:
        copy.start()
    return copies


def shifted(y, cols):
    col = iota(y.shape, 0)
    left = jnp.where(col == 0, 0.0, pltpu.roll(y, 1, 0))
    right = jnp.where(col == cols - 1, 0.0, pltpu.roll(y, cols - 1, 0))
    return jnp.concatenate([left, y, right], 1).astype(BF16)


def tile_hot(fields, width):
    return jnp.where((iota((fields, width), 1) - iota((fields, width), 0)) & (fields - 1) == 0, 1.0, 0.0).astype(BF16)


def fetched(pairs, sem, first=0):
    copies = [pltpu.make_async_copy(source, target, sem.at[first + n]) for n, (source, target) in enumerate(pairs)]
    for copy in copies:
        copy.start()
    return copies


def load_kernel(x_hbm, br_hbm, bs_hbm, bw_hbm, be_hbm, bt_hbm,
                last_ref, b_red_ref, b_mid_ref, b_wid_ref, b_ent_ref, b_str_ref, order_ref,
                br_ref, bs_ref, bw_ref, be_ref, bt_ref, sem):
    cols, wide = last_ref.shape
    large = fetched([(x_hbm.at[pl.ds(x_hbm.shape[0] - cols, cols)], last_ref)], sem)
    small = fetched([(br_hbm, br_ref), (bs_hbm, bs_ref), (bw_hbm, bw_ref), (be_hbm, be_ref), (bt_hbm, bt_ref)], sem, 1)
    in_f, mid_f, s4_f = wide // ORIENT, br_ref.shape[1], be_ref.shape[1]
    mid, s4 = mid_f * ORIENT, s4_f * ORIENT
    shift = s4_f.bit_length() - 1
    a, b = iota((s4, s4), 0), iota((s4, s4), 1)
    order_ref[...] = jnp.where(b == (a & (s4_f - 1)) * ORIENT + (a >> shift), 1.0, 0.0).astype(BF16)
    hot_mid, hot_s4, hot_wide = tile_hot(mid_f, mid), tile_hot(s4_f, s4), spread(in_f, 0, wide)
    for copy in small:
        copy.wait()
    b_red_ref[...] = bias_lanes(br_ref[...], hot_mid)
    b_mid_ref[...] = bias_lanes(bs_ref[...], hot_mid)
    b_ent_ref[...] = bias_lanes(be_ref[...], hot_s4)
    b_str_ref[...] = bias_lanes(bt_ref[...], hot_s4)
    b_wid_ref[...] = bias_lanes(bw_ref[...], hot_wide)
    large[0].wait()


def reducing(xs_ref, kr_ref, bias_ref, wr_ref, mids_ref, first_ref, second_ref):
    cols = first_ref.shape[0]
    strips = xs_ref.shape[0] // cols
    even = lax.axis_index("rows") % 2 == 0
    _, mid_f, in_f = kr_ref.shape
    def keep(at, block):
        wr_ref[at, :] = block
    unfold_in(kr_ref[...].reshape(mid_f * ORIENT, in_f), mid_f, keep)
    y = jnp.maximum(dot(xs_ref[...], wr_ref[...]) + bias_ref[...], 0.0)
    parts = [y[row * cols:(row + 1) * cols] for row in range(strips)]
    first_ref[...] = jnp.where(even, parts[strips - 2], parts[0]).astype(BF16)
    second_ref[...] = jnp.where(even, parts[0], parts[strips - 2]).astype(BF16)
    for row, part in enumerate(parts):
        mids_ref[pl.ds(row * cols, cols), :] = shifted(part, cols)


def strip_blocks(jobs, ws_ref, ww_ref, b_mid, b_wid, threes):
    twos = []
    for windows, _, _ in jobs:
        depth = windows[0].shape[1]
        acc = b_mid
        for dy in range(3):
            acc = acc + dot(windows[dy], ws_ref[pl.ds(dy * depth, depth), :])
        twos.append(jnp.maximum(acc, 0.0).astype(BF16))
    for two, (_, x, at) in zip(twos, jobs):
        for first in range(0, ww_ref.shape[1], 256):
            part = slice(first, first + 256)
            z = x(part).astype(F32) + dot(two, ww_ref[:, part]) + b_wid[:, part]
            threes[at, part] = jnp.maximum(z, 0.0).astype(BF16)


def entry_part(threes, we_ref, b_ent, at, first):
    cut = slice(first, first + 256)
    return jnp.maximum(dot(threes[at, :], we_ref[:, cut]) + b_ent[:, cut], 0.0)


def thirds(fours, threes, we_ref, b_ent, scales, cols, phases):
    half = cols // 2
    s4 = we_ref.shape[1]
    for first in range(0, s4, 256):
        for strip, scale in enumerate(scales):
            f = entry_part(threes, we_ref, b_ent, pl.ds(strip * cols, cols), first)
            if scale is not None:
                f = f * scale
            for g in range(2):
                fours[first // 128 + g, pl.ds(strip * cols, cols), :] = f[:, g * 128:(g + 1) * 128]
    col = iota((half, 128), 0)
    for strip in range(len(scales)):
        for g in range(s4 // 128):
            even = fours[g, pl.ds(strip * cols, half, stride=2), :]
            odd = fours[g, pl.ds(strip * cols + 1, half, stride=2), :]
            moved = jnp.where(col == 0, 0.0, pltpu.roll(odd, 1, 0))
            for n, value in enumerate((moved, even, odd)):
                phases[pl.ds(strip * half, half), pl.ds(n * s4 + g * 128, 128)] = value.astype(BF16)


def inner_kernel(xs_ref, mids_ref, b_mid_ref, b_wid_ref, b_ent_ref, ks_v, kw_ref, ke_ref, kt_v,
                 three_ref, ws_ref, ww_ref, we_ref, k2_ref, phases_ref,
                 flat_w, flat_s, flat_t, threes, fours, sem):
    in_f, s4_f, mid_f = ke_ref.shape[2], ke_ref.shape[1], kw_ref.shape[0]
    wide, s4, mid = in_f * ORIENT, s4_f * ORIENT, mid_f * ORIENT
    cols = phases_ref.shape[0]
    strips = xs_ref.shape[0] // cols
    flat_w[...] = kw_ref[...].astype(F32).reshape(mid, in_f)
    kw = jnp.concatenate([flat_w[pl.ds(u, mid_f, stride=ORIENT), :] for u in range(ORIENT)], 0).astype(BF16)
    for first in range(0, wide, 256):
        ww_ref[:, pl.ds(first, 256)] = turned(dot(kw, spread(in_f, first, 256)), mid_f).astype(BF16)
    def keep(at, block):
        we_ref[at, :] = block
    unfold_in(ke_ref[...].reshape(s4, in_f), s4_f, keep)

    lane = iota((1, 128), 1)
    for tap in range(9):
        flat_s[pl.ds(tap * mid, mid), :mid_f] = ks_v[tap].astype(F32).reshape(mid, mid_f)
    piece = lambda tap, u: flat_s[pl.ds(tap * mid + u % ORIENT, mid_f, stride=ORIENT), :]
    low = jnp.broadcast_to(lane < mid_f, (mid_f, 128))
    half = jnp.broadcast_to(lane < 2 * mid_f, (mid_f, 128))
    pairs = {}
    for tap in range(9):
        for u in range(ORIENT):
            pairs[tap, u] = jnp.where(low, piece(tap, u), pltpu.roll(piece(back_tap(tap, 1), u - 1), mid_f, 1))
    for tap in range(9):
        for u in range(ORIENT):
            quad = jnp.where(half, pairs[tap, u], pltpu.roll(pairs[back_tap(tap, 2), (u - 2) % ORIENT], 2 * mid_f, 1)).astype(BF16)
            ws_ref[pl.ds(tap * mid + u * mid_f, mid_f), :128] = quad
            ahead = back_tap(tap, -4)
            ws_ref[pl.ds(ahead * mid + (u + 4) % ORIENT * mid_f, mid_f), 128:] = quad

    for tap in range(9):
        flat_t[pl.ds(tap * s4, s4), :s4_f] = kt_v[tap].astype(F32).reshape(s4, s4_f)
    piece_t = lambda tap, u: flat_t[pl.ds(tap * s4 + u % ORIENT, s4_f, stride=ORIENT), :]
    low_t = jnp.broadcast_to(lane < s4_f, (s4_f, 128))
    for tap in range(9):
        for u in range(ORIENT):
            pair = jnp.where(low_t, piece_t(tap, u), pltpu.roll(piece_t(back_tap(tap, 1), u - 1), s4_f, 1))
            k2_ref[pl.ds(tap * s4 + u * s4_f, s4_f), :] = pair.astype(BF16)

    inner = strips - 2
    strip_of = lambda row: mids_ref[pl.ds(row * cols, cols), :]
    jobs = [([strip_of(row + dy) for dy in range(3)], lambda part, row=row: xs_ref[pl.ds((row + 1) * cols, cols), part],
             pl.ds(row * cols, cols)) for row in range(inner)]
    strip_blocks(jobs, ws_ref, ww_ref, b_mid_ref[...], b_wid_ref[...], threes)
    out = pltpu.make_async_copy(threes, three_ref.at[pl.ds(cols, inner * cols)], sem.at[0])
    out.start()
    thirds(fours, threes, we_ref, b_ent_ref[...], [None] * inner, cols, phases_ref)
    out.wait()


def edge_kernel(last_ref, first_ref, second_ref, xs_ref, wr_ref, bias_ref, b_mid_ref, b_wid_ref, b_ent_ref, b_str_ref, order_ref,
                mids_ref, ws_ref, ww_ref, we_ref, k2_ref, inner_ref, kept_ref,
                three_ref, four_ref, halo, threes, fours, phases, sem):
    place, count = lax.axis_index("rows"), lax.axis_size("rows")
    even = lax.axis_index("rows") % 2 == 0
    cols = first_ref.shape[0]
    half = cols // 2
    strips = xs_ref.shape[0] // cols
    wide, mid, s4 = xs_ref.shape[1], wr_ref.shape[1], we_ref.shape[1]
    not_first = jnp.where(place == 0, 0.0, 1.0)
    not_last = jnp.where(place == count - 1, 0.0, 1.0)
    strip_of = lambda row: mids_ref[pl.ds(row * cols, cols), :]
    got = [first_ref[...].astype(F32), second_ref[...].astype(F32)]
    last = strips - 1
    b_mid, b_wid, b_ent = b_mid_ref[...], b_wid_ref[...], b_ent_ref[...]
    halo[0] = shifted(jnp.where(even, got[1], got[0]) * not_first, cols)
    halo[2] = shifted(jnp.where(even, got[0], got[1]) * not_last, cols)
    halo[1] = shifted(jnp.maximum(dot(last_ref[...], wr_ref[...]) + bias_ref[...], 0.0) * not_first, cols)
    below = [strip_of(0), strip_of(1)] if last > 1 else [strip_of(0), halo[2]]
    jobs = [
        ([halo[0], halo[1], strip_of(0)], lambda part: last_ref[:, part], pl.ds(0, cols)),
        ([halo[1], *below], lambda part: xs_ref[pl.ds(0, cols), part], pl.ds(cols, cols)),
        ([strip_of(last - 1), strip_of(last), halo[2]], lambda part: xs_ref[pl.ds(last * cols, cols), part], pl.ds(2 * cols, cols)),
    ]
    strip_blocks(jobs, ws_ref, ww_ref, b_mid, b_wid, threes)
    outs = [
        pltpu.make_async_copy(threes.at[pl.ds(cols, cols)], three_ref.at[pl.ds(0, cols)], sem.at[0]),
        pltpu.make_async_copy(threes.at[pl.ds(2 * cols, cols)], three_ref.at[pl.ds(last * cols, cols)], sem.at[1]),
    ]
    for out in outs:
        out.start()
    thirds(fours, threes, we_ref, b_ent, [not_first, None, None], cols, phases)

    def rows_of(row, dx):
        cut = slice(dx * s4, (dx + 1) * s4)
        if row < 1:
            return phases[pl.ds((row + 1) * half, half), cut]
        if row == last:
            return phases[pl.ds(2 * half, half), cut]
        return inner_ref[pl.ds((row - 1) * half, half), cut]

    def filter_tile(tap, pair):
        halves = []
        for j in (2 * pair, 2 * pair + 1):
            source = back_tap(tap, 2 * j)
            halves.append(rows_rolled(k2_ref[pl.ds(source * s4, s4), :], 128 * j))
        return jnp.concatenate(halves, 1)

    lhs = []
    for tap in range(9):
        dy, dx = divmod(tap, 3)
        lhs.append(jnp.concatenate([rows_of(2 * q + dy - 1, dx) for q in range(strips // 2)], 0))
    results = []
    for pair in range(s4 // 256):
        acc = b_str_ref[:, pair * 256:(pair + 1) * 256]
        for tap in range(9):
            acc = acc + dot(lhs[tap], filter_tile(tap, pair))
        results.append(jnp.maximum(acc, 0.0).astype(BF16))
    four_ref[...] = dot(jnp.concatenate(results, 1), order_ref[...]).astype(BF16)
    for out in outs:
        out.wait()


def swaps(groups, count):
    near, far = [], []
    for group in range(groups):
        for row in range(count):
            me = group * count + row
            if row ^ 1 < count:
                near.append((me, group * count + (row ^ 1)))
            other = row - 1 if row % 2 == 0 else row + 1
            if 0 <= other < count:
                far.append((me, group * count + other))
            elif group ^ 1 < groups:
                far.append((me, (group ^ 1) * count + row))
    return near, far


def shards(scene_map, reduce_kernel, reduce_bias, spatial_kernel, spatial_bias, widen_kernel, widen_bias,
           entry_kernel, entry_bias, stride_kernel, stride_bias):
    count = lax.axis_size("rows")
    strips, cols, wide = scene_map.shape
    mid_f, s4_f = reduce_kernel.shape[2], entry_kernel.shape[2]
    mid, s4 = mid_f * ORIENT, s4_f * ORIENT
    own, half = strips * cols, cols // 2
    hbm = pl.BlockSpec(memory_space=pl.ANY)
    vmem = pl.BlockSpec(memory_space=pltpu.VMEM)
    dma = pltpu.SemaphoreType.DMA
    limit = lambda mib: pltpu.CompilerParams(vmem_limit_bytes=mib << 20)

    pinned = lambda *arrays: [pltpu.with_memory_space_constraint(a, pltpu.HBM) for a in arrays]
    scene = scene_map.reshape(own, wide)
    work = lambda flops: pl.CostEstimate(flops=flops, transcendentals=0, bytes_accessed=1 << 22)
    last, b_reduce, *known = pl.pallas_call(
        load_kernel,
        out_shape=[
            pltpu.VMEM((cols, wide), BF16),
            pltpu.VMEM((1, mid), F32),
            pltpu.VMEM((1, mid), F32),
            pltpu.VMEM((1, wide), F32),
            pltpu.VMEM((1, s4), F32),
            pltpu.VMEM((1, s4), F32),
            pltpu.VMEM((s4, s4), BF16),
        ],
        in_specs=[hbm] * 6,
        out_specs=[vmem] * 7,
        scratch_shapes=[
            pltpu.VMEM((1, mid_f), F32),
            pltpu.VMEM((1, mid_f), F32),
            pltpu.VMEM((1, wide // ORIENT), F32),
            pltpu.VMEM((1, s4_f), F32),
            pltpu.VMEM((1, s4_f), F32),
            dma((6,)),
        ],
        cost_estimate=work(2 * 10**9),
        compiler_params=limit(16),
        name="load",
    )(*pinned(scene, reduce_bias[None], spatial_bias[None], widen_bias[None], entry_bias[None], stride_bias[None]))
    b_mid, b_wid, b_ent = known[:3]
    last = lax.ppermute(last, "rows", [(i, (i + 1) % count) for i in range(count)])
    w_reduce, mids, first, second = pl.pallas_call(
        reducing,
        out_shape=[
            pltpu.VMEM((wide, mid), BF16),
            pltpu.VMEM((own, 3 * mid), BF16),
            pltpu.VMEM((cols, mid), BF16),
            pltpu.VMEM((cols, mid), BF16),
        ],
        in_specs=[vmem] * 3,
        out_specs=[vmem] * 4,
        cost_estimate=work(2 * 10**9),
        compiler_params=limit(16),
        name="reduce",
    )(scene, reduce_kernel.transpose(1, 2, 0), b_reduce)
    near, far = swaps(lax.axis_size("groups"), count)
    first = lax.ppermute(first, ("groups", "rows"), near)
    second = lax.ppermute(second, ("groups", "rows"), far)

    three, *kept, phases = pl.pallas_call(
        inner_kernel,
        out_shape=[
            jax.ShapeDtypeStruct((own, wide), BF16),
            pltpu.VMEM((9 * mid, mid), BF16),
            pltpu.VMEM((mid, wide), BF16),
            pltpu.VMEM((wide, s4), BF16),
            pltpu.VMEM((9 * s4, 128), BF16),
            pltpu.VMEM(((strips - 2) * half, 3 * s4), BF16),
        ],
        in_specs=[vmem] * 9,
        out_specs=[hbm] + [vmem] * 5,
        scratch_shapes=[
            pltpu.VMEM((mid, wide // ORIENT), F32),
            pltpu.VMEM((9 * mid, 128), F32),
            pltpu.VMEM((9 * s4, 128), F32),
            pltpu.VMEM(((strips - 2) * cols, wide), BF16),
            pltpu.VMEM((s4 // 128, (strips - 2) * cols, 128), F32),
            dma((1,)),
        ],
        compiler_params=limit(28),
        name="inner",
    )(scene, mids, b_mid, b_wid, b_ent, spatial_kernel, widen_kernel, entry_kernel.transpose(1, 2, 0), stride_kernel)

    operands = [last, first, second, scene, w_reduce, b_reduce, *known, mids, *kept, phases, three]
    three, four = pl.pallas_call(
        edge_kernel,
        out_shape=[
            jax.ShapeDtypeStruct((own, wide), BF16),
            jax.ShapeDtypeStruct((strips // 2 * half, s4), BF16),
        ],
        in_specs=[vmem] * (len(operands) - 1) + [hbm],
        out_specs=[hbm, vmem],
        input_output_aliases={len(operands) - 1: 0},
        scratch_shapes=[
            pltpu.VMEM((3, cols, 3 * mid), BF16),
            pltpu.VMEM((3 * cols, wide), BF16),
            pltpu.VMEM((s4 // 128, 3 * cols, 128), F32),
            pltpu.VMEM((3 * half, 3 * s4), BF16),
            dma((2,)),
        ],
        compiler_params=limit(28),
        name="edge",
    )(*operands)
    return three.reshape(strips, cols, wide), four.reshape(strips // 2, half, s4)


def solution(mesh):
    rows = P(("groups", "rows"), None, None)
    return jax.shard_map(shards, mesh=mesh, in_specs=(rows,) + (P(),) * 10, out_specs=(rows, rows), check_vma=False)
```

```python
import functools

import jax
import jax.numpy as jnp
from jax import lax
from jax.experimental import pallas as pl
from jax.experimental.pallas import tpu as pltpu
from jax.sharding import PartitionSpec as P

ORIENT = 8
BLOCK = 128
CYCLE_TAPS = [0, 1, 2, 5, 8, 7, 6, 3]
BF16, F32 = jnp.bfloat16, jnp.float32
NT = (((1,), (1,)), ((), ()))


def back_tap(tap, turn):
    if tap == 4:
        return 4
    return CYCLE_TAPS[(CYCLE_TAPS.index(tap) - turn) % ORIENT]


def iota(shape, dim):
    return lax.broadcasted_iota(jnp.int32, shape, dim)


def dot(a, b):
    return jnp.dot(a, b, preferred_element_type=F32)


def dot_nt(a, b):
    return lax.dot_general(a, b, NT, preferred_element_type=F32)


def rows_rolled(x, by):
    by %= x.shape[0]
    if by == 0:
        return x
    return jnp.concatenate([x[x.shape[0] - by:], x[:x.shape[0] - by]], 0)


def spread(fields, first, width):
    lead = iota((fields, width), 1) + first - ORIENT * iota((fields, width), 0)
    return jnp.where(lead & -ORIENT == 0, 1.0, 0.0).astype(BF16)


def turned(blocks, block):
    lane = iota((1, blocks.shape[1]), 1)
    for bit in (1, 2, 4):
        take = jnp.broadcast_to(lane & bit, blocks.shape) != 0
        blocks = jnp.where(take, rows_rolled(blocks, bit * block), blocks)
    return blocks


def unfold_in(kernel, fields, store):
    inputs = kernel.shape[1]
    base = jnp.concatenate([kernel[(-r) % ORIENT * fields:((-r) % ORIENT + 1) * fields] for r in range(ORIENT)], 0)
    base, other = base.T, rows_rolled(base, fields).T
    for first in range(0, inputs * ORIENT, 128):
        lead = iota((128, inputs), 0) + first - ORIENT * iota((128, inputs), 1)
        hot = jnp.where(lead & -ORIENT == 0, 1.0, 0.0).astype(BF16)
        row = iota((128, fields * ORIENT), 0)
        block = jnp.where(row & 1 != 0, dot(hot, other), dot(hot, base))
        for bit in (2, 4):
            block = jnp.where(row & bit != 0, pltpu.roll(block, bit * fields, 1), block)
        store(pl.ds(first, 128), block.astype(BF16))


def bias_lanes(bias, hot):
    first = bias.astype(BF16)
    rest = bias - first.astype(F32)
    second = rest.astype(BF16)
    third = (rest - second.astype(F32)).astype(BF16)
    parts = [dot(jnp.broadcast_to(p, (16,) + p.shape[1:]), hot)[:1] for p in (first, second, third)]
    return parts[0] + parts[1] + parts[2]


def fetched(pairs, sem, first=0):
    copies = [pltpu.make_async_copy(source, target, sem.at[first + n]) for n, (source, target) in enumerate(pairs)]
    for copy in copies:
        copy.start()
    return copies


def shifted(y, cols):
    col = iota(y.shape, 0)
    left = jnp.where(col == 0, 0.0, pltpu.roll(y, 1, 0))
    right = jnp.where(col == cols - 1, 0.0, pltpu.roll(y, cols - 1, 0))
    return jnp.concatenate([left, y, right], 1).astype(BF16)


def tile_hot(fields, width):
    return jnp.where((iota((fields, width), 1) - iota((fields, width), 0)) & (fields - 1) == 0, 1.0, 0.0).astype(BF16)


def fetched(pairs, sem, first=0):
    copies = [pltpu.make_async_copy(source, target, sem.at[first + n]) for n, (source, target) in enumerate(pairs)]
    for copy in copies:
        copy.start()
    return copies


def load_kernel(x_hbm, last_ref, sem):
    cols = last_ref.shape[0]
    cut, parts = cols // 4, []
    for n in range(4):
        parts.append((x_hbm.at[pl.ds(x_hbm.shape[0] - cols + n * cut, cut)], last_ref.at[pl.ds(n * cut, cut)]))
    for copy in fetched(parts, sem):
        copy.wait()


def reducing(xs_ref, kr_ref, br_ref, wr_ref, bias_ref, mids_ref, first_ref, second_ref):
    cols = first_ref.shape[0]
    strips = xs_ref.shape[0] // cols
    even = lax.axis_index("rows") % 2 == 0
    _, mid_f, in_f = kr_ref.shape
    def keep(at, block):
        wr_ref[at, :] = block
    unfold_in(kr_ref[...].reshape(mid_f * ORIENT, in_f), mid_f, keep)
    bias = bias_lanes(br_ref[...], tile_hot(mid_f, mid_f * ORIENT))
    bias_ref[...] = bias
    y = jnp.maximum(dot(xs_ref[...], wr_ref[...]) + bias, 0.0)
    parts = [y[row * cols:(row + 1) * cols] for row in range(strips)]
    first_ref[...] = jnp.where(even, parts[0], parts[strips - 2]).astype(BF16)
    second_ref[...] = jnp.where(even, parts[strips - 2], parts[0]).astype(BF16)
    for row, part in enumerate(parts):
        mids_ref[pl.ds(row * cols, cols), :] = shifted(part, cols)


def column_sum(windows, ws_ref, acc):
    for dy, window in windows.items():
        depth = window.shape[1]
        acc = acc + dot(window, ws_ref[pl.ds(dy * depth, depth), :])
    return acc


def strip_blocks(jobs, ws_ref, ww_ref, b_wid, threes):
    twos = []
    for (windows, start), _, _ in jobs:
        acc = column_sum(windows, ws_ref, start)
        twos.append(jnp.maximum(acc, 0.0).astype(BF16))
    for two, (_, x, at) in zip(twos, jobs):
        for first in range(0, ww_ref.shape[1], 256):
            part = slice(first, first + 256)
            z = x(part).astype(F32) + dot(two, ww_ref[:, part]) + b_wid[:, part]
            threes[at, part] = jnp.maximum(z, 0.0).astype(BF16)


def entry_part(threes, we_ref, b_ent, at, first):
    cut = slice(first, first + 256)
    return jnp.maximum(dot(threes[at, :], we_ref[:, cut]) + b_ent[:, cut], 0.0)


def thirds(fours, threes, we_ref, b_ent, scales, cols, phases):
    half = cols // 2
    s4 = we_ref.shape[1]
    for first in range(0, s4, 256):
        for strip, scale in enumerate(scales):
            f = entry_part(threes, we_ref, b_ent, pl.ds(strip * cols, cols), first)
            if scale is not None:
                f = f * scale
            for g in range(2):
                fours[first // 128 + g, pl.ds(strip * cols, cols), :] = f[:, g * 128:(g + 1) * 128]
    col = iota((half, 128), 0)
    for strip in range(len(scales)):
        for g in range(s4 // 128):
            even = fours[g, pl.ds(strip * cols, half, stride=2), :]
            odd = fours[g, pl.ds(strip * cols + 1, half, stride=2), :]
            moved = jnp.where(col == 0, 0.0, pltpu.roll(odd, 1, 0))
            for n, value in enumerate((moved, even, odd)):
                phases[pl.ds(strip * half, half), pl.ds(n * s4 + g * 128, 128)] = value.astype(BF16)


def inner_kernel(xs_ref, mids_ref, bs_ref, bw_ref, be_ref, bt_ref, ks_v, kw_ref, ke_ref, kt_v,
                 three_ref, ws_ref, ww_ref, we_ref, k2_ref, b_mid_ref, b_wid_ref, b_ent_ref, b_str_ref, order_ref, begun_ref, phases_ref,
                 flat_w, flat_s, flat_t, threes, fours, sem):
    in_f, s4_f, mid_f = ke_ref.shape[2], ke_ref.shape[1], kw_ref.shape[0]
    wide, s4, mid = in_f * ORIENT, s4_f * ORIENT, mid_f * ORIENT
    cols = phases_ref.shape[0]
    strips = xs_ref.shape[0] // cols
    flat_w[...] = kw_ref[...].astype(F32).reshape(mid, in_f)
    kw = jnp.concatenate([flat_w[pl.ds(u, mid_f, stride=ORIENT), :] for u in range(ORIENT)], 0).astype(BF16)
    shift = s4_f.bit_length() - 1
    a, b = iota((s4, s4), 0), iota((s4, s4), 1)
    order_ref[...] = jnp.where(b == (a & (s4_f - 1)) * ORIENT + (a >> shift), 1.0, 0.0).astype(BF16)
    hot_s4 = tile_hot(s4_f, s4)
    b_mid_ref[...] = bias_lanes(bs_ref[...], tile_hot(mid_f, mid))
    b_ent_ref[...] = bias_lanes(be_ref[...], hot_s4)
    b_str_ref[...] = bias_lanes(bt_ref[...], hot_s4)
    for first in range(0, wide, 256):
        hot = spread(in_f, first, 256)
        ww_ref[:, pl.ds(first, 256)] = turned(dot(kw, hot), mid_f).astype(BF16)
        b_wid_ref[:, pl.ds(first, 256)] = bias_lanes(bw_ref[...], hot)
    def keep(at, block):
        we_ref[at, :] = block
    unfold_in(ke_ref[...].reshape(s4, in_f), s4_f, keep)

    lane = iota((1, 128), 1)
    for tap in range(9):
        flat_s[pl.ds(tap * mid, mid), :mid_f] = ks_v[tap].astype(F32).reshape(mid, mid_f)
    piece = lambda tap, u: flat_s[pl.ds(tap * mid + u % ORIENT, mid_f, stride=ORIENT), :]
    low = jnp.broadcast_to(lane < mid_f, (mid_f, 128))
    half = jnp.broadcast_to(lane < 2 * mid_f, (mid_f, 128))
    pairs = {}
    for tap in range(9):
        for u in range(ORIENT):
            pairs[tap, u] = jnp.where(low, piece(tap, u), pltpu.roll(piece(back_tap(tap, 1), u - 1), mid_f, 1))
    for tap in range(9):
        for u in range(ORIENT):
            quad = jnp.where(half, pairs[tap, u], pltpu.roll(pairs[back_tap(tap, 2), (u - 2) % ORIENT], 2 * mid_f, 1)).astype(BF16)
            ws_ref[pl.ds(tap * mid + u * mid_f, mid_f), :128] = quad
            ahead = back_tap(tap, -4)
            ws_ref[pl.ds(ahead * mid + (u + 4) % ORIENT * mid_f, mid_f), 128:] = quad

    for tap in range(9):
        flat_t[pl.ds(tap * s4, s4), :s4_f] = kt_v[tap].astype(F32).reshape(s4, s4_f)
    piece_t = lambda tap, u: flat_t[pl.ds(tap * s4 + u % ORIENT, s4_f, stride=ORIENT), :]
    low_t = jnp.broadcast_to(lane < s4_f, (s4_f, 128))
    for tap in range(9):
        for u in range(ORIENT):
            pair = jnp.where(low_t, piece_t(tap, u), pltpu.roll(piece_t(back_tap(tap, 1), u - 1), s4_f, 1))
            k2_ref[pl.ds(tap * s4 + u * s4_f, s4_f), :] = pair.astype(BF16)

    inner = strips - 2
    strip_of = lambda row: mids_ref[pl.ds(row * cols, cols), :]
    b_mid = b_mid_ref[...]
    jobs = [(({dy: strip_of(row + dy) for dy in range(3)}, b_mid), lambda part, row=row: xs_ref[pl.ds((row + 1) * cols, cols), part],
             pl.ds(row * cols, cols)) for row in range(inner)]
    strip_blocks(jobs, ws_ref, ww_ref, b_wid_ref[...], threes)
    out = pltpu.make_async_copy(threes, three_ref.at[pl.ds(cols, inner * cols)], sem.at[0])
    out.start()
    begun_ref[0] = column_sum({1: strip_of(0), 2: strip_of(1)}, ws_ref, b_mid)
    begun_ref[1] = column_sum({0: strip_of(inner), 1: strip_of(inner + 1)}, ws_ref, b_mid)
    thirds(fours, threes, we_ref, b_ent_ref[...], [None] * inner, cols, phases_ref)
    out.wait()


def edge_kernel(last_ref, first_ref, second_ref, xs_ref, wr_ref, bias_ref, mids_ref, ws_ref, ww_ref, we_ref, k2_ref,
                b_mid_ref, b_wid_ref, b_ent_ref, b_str_ref, order_ref, begun_ref, inner_ref, kept_ref,
                three_ref, four_ref, halo, threes, fours, phases, sem):
    place, count = lax.axis_index("rows"), lax.axis_size("rows")
    even = lax.axis_index("rows") % 2 == 0
    cols = first_ref.shape[0]
    half = cols // 2
    strips = xs_ref.shape[0] // cols
    wide, mid, s4 = xs_ref.shape[1], wr_ref.shape[1], we_ref.shape[1]
    not_first = jnp.where(place == 0, 0.0, 1.0)
    not_last = jnp.where(place == count - 1, 0.0, 1.0)
    strip_of = lambda row: mids_ref[pl.ds(row * cols, cols), :]
    got = [first_ref[...].astype(F32), second_ref[...].astype(F32)]
    last = strips - 1
    b_mid, b_wid, b_ent = b_mid_ref[...], b_wid_ref[...], b_ent_ref[...]
    halo[0] = shifted(jnp.where(even, got[0], got[1]) * not_first, cols)
    halo[2] = shifted(jnp.where(even, got[1], got[0]) * not_last, cols)
    halo[1] = shifted(jnp.maximum(dot(last_ref[...], wr_ref[...]) + bias_ref[...], 0.0) * not_first, cols)
    jobs = [
        (({0: halo[0], 1: halo[1], 2: strip_of(0)}, b_mid), lambda part: last_ref[:, part], pl.ds(0, cols)),
        (({0: halo[1]}, begun_ref[0]), lambda part: xs_ref[pl.ds(0, cols), part], pl.ds(cols, cols)),
        (({2: halo[2]}, begun_ref[1]), lambda part: xs_ref[pl.ds(last * cols, cols), part], pl.ds(2 * cols, cols)),
    ]
    strip_blocks(jobs, ws_ref, ww_ref, b_wid, threes)
    outs = [
        pltpu.make_async_copy(threes.at[pl.ds(cols, cols)], three_ref.at[pl.ds(0, cols)], sem.at[0]),
        pltpu.make_async_copy(threes.at[pl.ds(2 * cols, cols)], three_ref.at[pl.ds(last * cols, cols)], sem.at[1]),
    ]
    for out in outs:
        out.start()
    thirds(fours, threes, we_ref, b_ent, [not_first, None, None], cols, phases)

    def rows_of(row, dx):
        cut = slice(dx * s4, (dx + 1) * s4)
        if row < 1:
            return phases[pl.ds((row + 1) * half, half), cut]
        if row == last:
            return phases[pl.ds(2 * half, half), cut]
        return inner_ref[pl.ds((row - 1) * half, half), cut]

    def filter_tile(tap, pair):
        halves = []
        for j in (2 * pair, 2 * pair + 1):
            source = back_tap(tap, 2 * j)
            halves.append(rows_rolled(k2_ref[pl.ds(source * s4, s4), :], 128 * j))
        return jnp.concatenate(halves, 1)

    lhs = []
    for tap in range(9):
        dy, dx = divmod(tap, 3)
        lhs.append(jnp.concatenate([rows_of(2 * q + dy - 1, dx) for q in range(strips // 2)], 0))
    results = []
    for pair in range(s4 // 256):
        acc = b_str_ref[:, pair * 256:(pair + 1) * 256]
        for tap in range(9):
            acc = acc + dot(lhs[tap], filter_tile(tap, pair))
        results.append(jnp.maximum(acc, 0.0).astype(BF16))
    four_ref[...] = dot(jnp.concatenate(results, 1), order_ref[...]).astype(BF16)
    for out in outs:
        out.wait()


def swaps(groups, count):
    near, far = [], []
    for group in range(groups):
        for row in range(count):
            me = group * count + row
            if row ^ 1 < count:
                near.append((me, group * count + (row ^ 1)))
            other = row - 1 if row % 2 == 0 else row + 1
            if 0 <= other < count:
                far.append((me, group * count + other))
            elif group ^ 1 < groups:
                far.append((me, (group ^ 1) * count + row))
    return near, far


def shards(scene_map, reduce_kernel, reduce_bias, spatial_kernel, spatial_bias, widen_kernel, widen_bias,
           entry_kernel, entry_bias, stride_kernel, stride_bias):
    count = lax.axis_size("rows")
    strips, cols, wide = scene_map.shape
    mid_f, s4_f = reduce_kernel.shape[2], entry_kernel.shape[2]
    mid, s4 = mid_f * ORIENT, s4_f * ORIENT
    own, half = strips * cols, cols // 2
    hbm = pl.BlockSpec(memory_space=pl.ANY)
    vmem = pl.BlockSpec(memory_space=pltpu.VMEM)
    dma = pltpu.SemaphoreType.DMA
    limit = lambda mib: pltpu.CompilerParams(vmem_limit_bytes=mib << 20)

    pinned = lambda *arrays: [pltpu.with_memory_space_constraint(a, pltpu.HBM) for a in arrays]
    scene = scene_map.reshape(own, wide)
    work = lambda flops: pl.CostEstimate(flops=flops, transcendentals=0, bytes_accessed=1 << 22)
    last = pl.pallas_call(
        load_kernel,
        out_shape=pltpu.VMEM((cols, wide), BF16),
        in_specs=[hbm],
        out_specs=vmem,
        scratch_shapes=[dma((4,))],
        cost_estimate=work(2 * 10**9),
        compiler_params=limit(16),
        name="load",
    )(*pinned(scene))
    last = lax.ppermute(last, "rows", [(i, (i + 1) % count) for i in range(count)])
    w_reduce, b_reduce, mids, first, second = pl.pallas_call(
        reducing,
        out_shape=[
            pltpu.VMEM((wide, mid), BF16),
            pltpu.VMEM((1, mid), F32),
            pltpu.VMEM((own, 3 * mid), BF16),
            pltpu.VMEM((cols, mid), BF16),
            pltpu.VMEM((cols, mid), BF16),
        ],
        in_specs=[vmem] * 3,
        out_specs=[vmem] * 5,
        cost_estimate=work(2 * 10**9),
        compiler_params=limit(16),
        name="reduce",
    )(scene, reduce_kernel.transpose(1, 2, 0), reduce_bias[None])
    near, far = swaps(lax.axis_size("groups"), count)
    first = lax.ppermute(first, ("groups", "rows"), far)
    second = lax.ppermute(second, ("groups", "rows"), near)

    three, *kept, phases = pl.pallas_call(
        inner_kernel,
        out_shape=[
            jax.ShapeDtypeStruct((own, wide), BF16),
            pltpu.VMEM((9 * mid, mid), BF16),
            pltpu.VMEM((mid, wide), BF16),
            pltpu.VMEM((wide, s4), BF16),
            pltpu.VMEM((9 * s4, 128), BF16),
            pltpu.VMEM((1, mid), F32),
            pltpu.VMEM((1, wide), F32),
            pltpu.VMEM((1, s4), F32),
            pltpu.VMEM((1, s4), F32),
            pltpu.VMEM((s4, s4), BF16),
            pltpu.VMEM((2, cols, mid), F32),
            pltpu.VMEM(((strips - 2) * half, 3 * s4), BF16),
        ],
        in_specs=[vmem] * 10,
        out_specs=[hbm] + [vmem] * 11,
        scratch_shapes=[
            pltpu.VMEM((mid, wide // ORIENT), F32),
            pltpu.VMEM((9 * mid, 128), F32),
            pltpu.VMEM((9 * s4, 128), F32),
            pltpu.VMEM(((strips - 2) * cols, wide), BF16),
            pltpu.VMEM((s4 // 128, (strips - 2) * cols, 128), F32),
            dma((1,)),
        ],
        compiler_params=limit(28),
        name="inner",
    )(scene, mids, spatial_bias[None], widen_bias[None], entry_bias[None], stride_bias[None], spatial_kernel, widen_kernel, entry_kernel.transpose(1, 2, 0), stride_kernel)

    operands = [last, first, second, scene, w_reduce, b_reduce, mids, *kept, phases, three]
    three, four = pl.pallas_call(
        edge_kernel,
        out_shape=[
            jax.ShapeDtypeStruct((own, wide), BF16),
            jax.ShapeDtypeStruct((strips // 2 * half, s4), BF16),
        ],
        in_specs=[vmem] * (len(operands) - 1) + [hbm],
        out_specs=[hbm, vmem],
        input_output_aliases={len(operands) - 1: 0},
        scratch_shapes=[
            pltpu.VMEM((3, cols, 3 * mid), BF16),
            pltpu.VMEM((3 * cols, wide), BF16),
            pltpu.VMEM((s4 // 128, 3 * cols, 128), F32),
            pltpu.VMEM((3 * half, 3 * s4), BF16),
            dma((2,)),
        ],
        compiler_params=limit(28),
        name="edge",
    )(*operands)
    return three.reshape(strips, cols, wide), four.reshape(strips // 2, half, s4)


def solution(mesh):
    rows = P(("groups", "rows"), None, None)
    return jax.shard_map(shards, mesh=mesh, in_specs=(rows,) + (P(),) * 10, out_specs=(rows, rows), check_vma=False)
```

```python
import functools

import jax
import jax.numpy as jnp
from jax import lax
from jax.experimental import pallas as pl
from jax.experimental.pallas import tpu as pltpu
from jax.sharding import PartitionSpec as P

ORIENT = 8
BLOCK = 128
CYCLE_TAPS = [0, 1, 2, 5, 8, 7, 6, 3]
BF16, F32 = jnp.bfloat16, jnp.float32
NT = (((1,), (1,)), ((), ()))


def back_tap(tap, turn):
    if tap == 4:
        return 4
    return CYCLE_TAPS[(CYCLE_TAPS.index(tap) - turn) % ORIENT]


def iota(shape, dim):
    return lax.broadcasted_iota(jnp.int32, shape, dim)


def dot(a, b):
    return jnp.dot(a, b, preferred_element_type=F32)


def dot_nt(a, b):
    return lax.dot_general(a, b, NT, preferred_element_type=F32)


def rows_rolled(x, by):
    by %= x.shape[0]
    if by == 0:
        return x
    return jnp.concatenate([x[x.shape[0] - by:], x[:x.shape[0] - by]], 0)


def spread(fields, first, width):
    lead = iota((fields, width), 1) + first - ORIENT * iota((fields, width), 0)
    return jnp.where(lead & -ORIENT == 0, 1.0, 0.0).astype(BF16)


def turned(blocks, block):
    lane = iota((1, blocks.shape[1]), 1)
    for bit in (1, 2, 4):
        take = jnp.broadcast_to(lane & bit, blocks.shape) != 0
        blocks = jnp.where(take, rows_rolled(blocks, bit * block), blocks)
    return blocks


def unfold_in(kernel, fields, store):
    inputs = kernel.shape[1]
    base = jnp.concatenate([kernel[(-r) % ORIENT * fields:((-r) % ORIENT + 1) * fields] for r in range(ORIENT)], 0)
    base, other = base.T, rows_rolled(base, fields).T
    for first in range(0, inputs * ORIENT, 128):
        lead = iota((128, inputs), 0) + first - ORIENT * iota((128, inputs), 1)
        hot = jnp.where(lead & -ORIENT == 0, 1.0, 0.0).astype(BF16)
        row = iota((128, fields * ORIENT), 0)
        block = jnp.where(row & 1 != 0, dot(hot, other), dot(hot, base))
        for bit in (2, 4):
            block = jnp.where(row & bit != 0, pltpu.roll(block, bit * fields, 1), block)
        store(pl.ds(first, 128), block.astype(BF16))


def bias_lanes(bias, hot):
    first = bias.astype(BF16)
    rest = bias - first.astype(F32)
    second = rest.astype(BF16)
    third = (rest - second.astype(F32)).astype(BF16)
    parts = [dot(jnp.broadcast_to(p, (16,) + p.shape[1:]), hot)[:1] for p in (first, second, third)]
    return parts[0] + parts[1] + parts[2]


def fetched(pairs, sem, first=0):
    copies = [pltpu.make_async_copy(source, target, sem.at[first + n]) for n, (source, target) in enumerate(pairs)]
    for copy in copies:
        copy.start()
    return copies


def shifted(y, cols):
    col = iota(y.shape, 0)
    left = jnp.where(col == 0, 0.0, pltpu.roll(y, 1, 0))
    right = jnp.where(col == cols - 1, 0.0, pltpu.roll(y, cols - 1, 0))
    return jnp.concatenate([left, y, right], 1).astype(BF16)


def tile_hot(fields, width):
    return jnp.where((iota((fields, width), 1) - iota((fields, width), 0)) & (fields - 1) == 0, 1.0, 0.0).astype(BF16)


def fetched(pairs, sem, first=0):
    copies = [pltpu.make_async_copy(source, target, sem.at[first + n]) for n, (source, target) in enumerate(pairs)]
    for copy in copies:
        copy.start()
    return copies


def load_kernel(x_hbm, last_ref, sem):
    cols = last_ref.shape[0]
    copy = pltpu.make_async_copy(x_hbm.at[pl.ds(x_hbm.shape[0] - cols, cols)], last_ref, sem)
    copy.start()
    copy.wait()


def reducing(xs_ref, kr_ref, br_ref, wr_ref, bias_ref, mids_ref, first_ref, second_ref):
    cols = first_ref.shape[0]
    strips = xs_ref.shape[0] // cols
    even = lax.axis_index("rows") % 2 == 0
    _, mid_f, in_f = kr_ref.shape
    def keep(at, block):
        wr_ref[at, :] = block
    unfold_in(kr_ref[...].reshape(mid_f * ORIENT, in_f), mid_f, keep)
    bias = bias_lanes(br_ref[...], tile_hot(mid_f, mid_f * ORIENT))
    bias_ref[...] = bias
    y = jnp.maximum(dot(xs_ref[...], wr_ref[...]) + bias, 0.0)
    parts = [y[row * cols:(row + 1) * cols] for row in range(strips)]
    first_ref[...] = jnp.where(even, parts[0], parts[strips - 2]).astype(BF16)
    second_ref[...] = jnp.where(even, parts[strips - 2], parts[0]).astype(BF16)
    for row, part in enumerate(parts):
        mids_ref[pl.ds(row * cols, cols), :] = shifted(part, cols)


def strip_blocks(jobs, ws_ref, ww_ref, b_mid, b_wid, threes):
    twos = []
    for windows, _, _ in jobs:
        depth = windows[0].shape[1]
        acc = b_mid
        for dy in range(3):
            acc = acc + dot(windows[dy], ws_ref[pl.ds(dy * depth, depth), :])
        twos.append(jnp.maximum(acc, 0.0).astype(BF16))
    for two, (_, x, at) in zip(twos, jobs):
        for first in range(0, ww_ref.shape[1], 256):
            part = slice(first, first + 256)
            z = x(part).astype(F32) + dot(two, ww_ref[:, part]) + b_wid[:, part]
            threes[at, part] = jnp.maximum(z, 0.0).astype(BF16)


def entry_part(threes, we_ref, b_ent, at, first):
    cut = slice(first, first + 256)
    return jnp.maximum(dot(threes[at, :], we_ref[:, cut]) + b_ent[:, cut], 0.0)


def thirds(fours, threes, we_ref, b_ent, scales, cols, phases):
    half = cols // 2
    s4 = we_ref.shape[1]
    for first in range(0, s4, 256):
        for strip, scale in enumerate(scales):
            f = entry_part(threes, we_ref, b_ent, pl.ds(strip * cols, cols), first)
            if scale is not None:
                f = f * scale
            for g in range(2):
                fours[first // 128 + g, pl.ds(strip * cols, cols), :] = f[:, g * 128:(g + 1) * 128]
    col = iota((half, 128), 0)
    for strip in range(len(scales)):
        for g in range(s4 // 128):
            even = fours[g, pl.ds(strip * cols, half, stride=2), :]
            odd = fours[g, pl.ds(strip * cols + 1, half, stride=2), :]
            moved = jnp.where(col == 0, 0.0, pltpu.roll(odd, 1, 0))
            for n, value in enumerate((moved, even, odd)):
                phases[pl.ds(strip * half, half), pl.ds(n * s4 + g * 128, 128)] = value.astype(BF16)


def inner_kernel(xs_ref, mids_ref, bs_ref, bw_ref, be_ref, bt_ref, ks_v, kw_ref, ke_ref, kt_v,
                 three_ref, ws_ref, ww_ref, we_ref, k2_ref, b_mid_ref, b_wid_ref, b_ent_ref, b_str_ref, order_ref, phases_ref,
                 flat_w, flat_s, flat_t, threes, fours, sem):
    in_f, s4_f, mid_f = ke_ref.shape[2], ke_ref.shape[1], kw_ref.shape[0]
    wide, s4, mid = in_f * ORIENT, s4_f * ORIENT, mid_f * ORIENT
    cols = phases_ref.shape[0]
    strips = xs_ref.shape[0] // cols
    flat_w[...] = kw_ref[...].astype(F32).reshape(mid, in_f)
    kw = jnp.concatenate([flat_w[pl.ds(u, mid_f, stride=ORIENT), :] for u in range(ORIENT)], 0).astype(BF16)
    shift = s4_f.bit_length() - 1
    a, b = iota((s4, s4), 0), iota((s4, s4), 1)
    order_ref[...] = jnp.where(b == (a & (s4_f - 1)) * ORIENT + (a >> shift), 1.0, 0.0).astype(BF16)
    hot_s4 = tile_hot(s4_f, s4)
    b_mid_ref[...] = bias_lanes(bs_ref[...], tile_hot(mid_f, mid))
    b_ent_ref[...] = bias_lanes(be_ref[...], hot_s4)
    b_str_ref[...] = bias_lanes(bt_ref[...], hot_s4)
    for first in range(0, wide, 256):
        hot = spread(in_f, first, 256)
        ww_ref[:, pl.ds(first, 256)] = turned(dot(kw, hot), mid_f).astype(BF16)
        b_wid_ref[:, pl.ds(first, 256)] = bias_lanes(bw_ref[...], hot)
    def keep(at, block):
        we_ref[at, :] = block
    unfold_in(ke_ref[...].reshape(s4, in_f), s4_f, keep)

    lane = iota((1, 128), 1)
    for tap in range(9):
        flat_s[pl.ds(tap * mid, mid), :mid_f] = ks_v[tap].astype(F32).reshape(mid, mid_f)
    piece = lambda tap, u: flat_s[pl.ds(tap * mid + u % ORIENT, mid_f, stride=ORIENT), :]
    low = jnp.broadcast_to(lane < mid_f, (mid_f, 128))
    half = jnp.broadcast_to(lane < 2 * mid_f, (mid_f, 128))
    pairs = {}
    for tap in range(9):
        for u in range(ORIENT):
            pairs[tap, u] = jnp.where(low, piece(tap, u), pltpu.roll(piece(back_tap(tap, 1), u - 1), mid_f, 1))
    for tap in range(9):
        for u in range(ORIENT):
            quad = jnp.where(half, pairs[tap, u], pltpu.roll(pairs[back_tap(tap, 2), (u - 2) % ORIENT], 2 * mid_f, 1)).astype(BF16)
            ws_ref[pl.ds(tap * mid + u * mid_f, mid_f), :128] = quad
            ahead = back_tap(tap, -4)
            ws_ref[pl.ds(ahead * mid + (u + 4) % ORIENT * mid_f, mid_f), 128:] = quad

    for tap in range(9):
        flat_t[pl.ds(tap * s4, s4), :s4_f] = kt_v[tap].astype(F32).reshape(s4, s4_f)
    piece_t = lambda tap, u: flat_t[pl.ds(tap * s4 + u % ORIENT, s4_f, stride=ORIENT), :]
    low_t = jnp.broadcast_to(lane < s4_f, (s4_f, 128))
    for tap in range(9):
        for u in range(ORIENT):
            pair = jnp.where(low_t, piece_t(tap, u), pltpu.roll(piece_t(back_tap(tap, 1), u - 1), s4_f, 1))
            k2_ref[pl.ds(tap * s4 + u * s4_f, s4_f), :] = pair.astype(BF16)

    inner = strips - 2
    strip_of = lambda row: mids_ref[pl.ds(row * cols, cols), :]
    jobs = [([strip_of(row + dy) for dy in range(3)], lambda part, row=row: xs_ref[pl.ds((row + 1) * cols, cols), part],
             pl.ds(row * cols, cols)) for row in range(inner)]
    strip_blocks(jobs, ws_ref, ww_ref, b_mid_ref[...], b_wid_ref[...], threes)
    out = pltpu.make_async_copy(threes, three_ref.at[pl.ds(cols, inner * cols)], sem.at[0])
    out.start()
    thirds(fours, threes, we_ref, b_ent_ref[...], [None] * inner, cols, phases_ref)
    out.wait()


def edge_kernel(last_ref, beside_ref, first_ref, second_ref, xs_ref, wr_ref, bias_ref, mids_ref, ws_ref, ww_ref, we_ref, k2_ref,
                b_mid_ref, b_wid_ref, b_ent_ref, b_str_ref, order_ref, inner_ref, kept_ref,
                three_ref, four_ref, halo, line, threes, fours, phases, sem):
    place, count = lax.axis_index("rows"), lax.axis_size("rows")
    even = lax.axis_index("rows") % 2 == 0
    cols = first_ref.shape[0]
    half = cols // 2
    strips = xs_ref.shape[0] // cols
    wide, mid, s4 = xs_ref.shape[1], wr_ref.shape[1], we_ref.shape[1]
    not_first = jnp.where(place == 0, 0.0, 1.0)
    not_last = jnp.where(place == count - 1, 0.0, 1.0)
    strip_of = lambda row: mids_ref[pl.ds(row * cols, cols), :]
    line[...] = jnp.where(even, last_ref[...], beside_ref[...])
    got = [first_ref[...].astype(F32), second_ref[...].astype(F32)]
    last = strips - 1
    b_mid, b_wid, b_ent = b_mid_ref[...], b_wid_ref[...], b_ent_ref[...]
    halo[0] = shifted(jnp.where(even, got[0], got[1]) * not_first, cols)
    halo[2] = shifted(jnp.where(even, got[1], got[0]) * not_last, cols)
    halo[1] = shifted(jnp.maximum(dot(line[...], wr_ref[...]) + bias_ref[...], 0.0) * not_first, cols)
    below = [strip_of(0), strip_of(1)] if last > 1 else [strip_of(0), halo[2]]
    jobs = [
        ([halo[0], halo[1], strip_of(0)], lambda part: line[:, part], pl.ds(0, cols)),
        ([halo[1], *below], lambda part: xs_ref[pl.ds(0, cols), part], pl.ds(cols, cols)),
        ([strip_of(last - 1), strip_of(last), halo[2]], lambda part: xs_ref[pl.ds(last * cols, cols), part], pl.ds(2 * cols, cols)),
    ]
    strip_blocks(jobs, ws_ref, ww_ref, b_mid, b_wid, threes)
    outs = [
        pltpu.make_async_copy(threes.at[pl.ds(cols, cols)], three_ref.at[pl.ds(0, cols)], sem.at[0]),
        pltpu.make_async_copy(threes.at[pl.ds(2 * cols, cols)], three_ref.at[pl.ds(last * cols, cols)], sem.at[1]),
    ]
    for out in outs:
        out.start()
    thirds(fours, threes, we_ref, b_ent, [not_first, None, None], cols, phases)

    def rows_of(row, dx):
        cut = slice(dx * s4, (dx + 1) * s4)
        if row < 1:
            return phases[pl.ds((row + 1) * half, half), cut]
        if row == last:
            return phases[pl.ds(2 * half, half), cut]
        return inner_ref[pl.ds((row - 1) * half, half), cut]

    def filter_tile(tap, pair):
        halves = []
        for j in (2 * pair, 2 * pair + 1):
            source = back_tap(tap, 2 * j)
            halves.append(rows_rolled(k2_ref[pl.ds(source * s4, s4), :], 128 * j))
        return jnp.concatenate(halves, 1)

    lhs = []
    for tap in range(9):
        dy, dx = divmod(tap, 3)
        lhs.append(jnp.concatenate([rows_of(2 * q + dy - 1, dx) for q in range(strips // 2)], 0))
    results = []
    for pair in range(s4 // 256):
        acc = b_str_ref[:, pair * 256:(pair + 1) * 256]
        for tap in range(9):
            acc = acc + dot(lhs[tap], filter_tile(tap, pair))
        results.append(jnp.maximum(acc, 0.0).astype(BF16))
    four_ref[...] = dot(jnp.concatenate(results, 1), order_ref[...]).astype(BF16)
    for out in outs:
        out.wait()


def swaps(groups, count):
    near, far = [], []
    for group in range(groups):
        for row in range(count):
            me = group * count + row
            if row ^ 1 < count:
                near.append((me, group * count + (row ^ 1)))
            other = row - 1 if row % 2 == 0 else row + 1
            if 0 <= other < count:
                far.append((me, group * count + other))
            elif group ^ 1 < groups:
                far.append((me, (group ^ 1) * count + row))
    return near, far


def odd_down(count):
    if count < 8 or count % 4:
        return [(i, (i + 1) % count) for i in range(count)]
    pairs = {i: i + 1 for i in range(count - 1)}
    for i in range(2, count - 4, 4):
        pairs[i] = i - 3 if i > 2 else 0
    pairs[count - 1] = count - 5
    return sorted(pairs.items())


def shards(scene_map, reduce_kernel, reduce_bias, spatial_kernel, spatial_bias, widen_kernel, widen_bias,
           entry_kernel, entry_bias, stride_kernel, stride_bias):
    count = lax.axis_size("rows")
    strips, cols, wide = scene_map.shape
    mid_f, s4_f = reduce_kernel.shape[2], entry_kernel.shape[2]
    mid, s4 = mid_f * ORIENT, s4_f * ORIENT
    own, half = strips * cols, cols // 2
    hbm = pl.BlockSpec(memory_space=pl.ANY)
    vmem = pl.BlockSpec(memory_space=pltpu.VMEM)
    dma = pltpu.SemaphoreType.DMA
    limit = lambda mib: pltpu.CompilerParams(vmem_limit_bytes=mib << 20)

    pinned = lambda *arrays: [pltpu.with_memory_space_constraint(a, pltpu.HBM) for a in arrays]
    scene = scene_map.reshape(own, wide)
    work = lambda flops: pl.CostEstimate(flops=flops, transcendentals=0, bytes_accessed=1 << 22)
    last = pl.pallas_call(
        load_kernel,
        out_shape=pltpu.VMEM((cols, wide), BF16),
        in_specs=[hbm],
        out_specs=vmem,
        scratch_shapes=[dma],
        cost_estimate=work(2 * 10**9),
        compiler_params=limit(16),
        name="load",
    )(*pinned(scene))
    near, far = swaps(lax.axis_size("groups"), count)
    beside = lax.ppermute(last, ("groups", "rows"), near)
    last = lax.ppermute(last, "rows", odd_down(count))
    w_reduce, b_reduce, mids, first, second = pl.pallas_call(
        reducing,
        out_shape=[
            pltpu.VMEM((wide, mid), BF16),
            pltpu.VMEM((1, mid), F32),
            pltpu.VMEM((own, 3 * mid), BF16),
            pltpu.VMEM((cols, mid), BF16),
            pltpu.VMEM((cols, mid), BF16),
        ],
        in_specs=[vmem] * 3,
        out_specs=[vmem] * 5,
        cost_estimate=work(2 * 10**9),
        compiler_params=limit(16),
        name="reduce",
    )(scene, reduce_kernel.transpose(1, 2, 0), reduce_bias[None])
    first = lax.ppermute(first, ("groups", "rows"), far)
    second = lax.ppermute(second, ("groups", "rows"), near)

    three, *kept, phases = pl.pallas_call(
        inner_kernel,
        out_shape=[
            jax.ShapeDtypeStruct((own, wide), BF16),
            pltpu.VMEM((9 * mid, mid), BF16),
            pltpu.VMEM((mid, wide), BF16),
            pltpu.VMEM((wide, s4), BF16),
            pltpu.VMEM((9 * s4, 128), BF16),
            pltpu.VMEM((1, mid), F32),
            pltpu.VMEM((1, wide), F32),
            pltpu.VMEM((1, s4), F32),
            pltpu.VMEM((1, s4), F32),
            pltpu.VMEM((s4, s4), BF16),
            pltpu.VMEM(((strips - 2) * half, 3 * s4), BF16),
        ],
        in_specs=[vmem] * 10,
        out_specs=[hbm] + [vmem] * 10,
        scratch_shapes=[
            pltpu.VMEM((mid, wide // ORIENT), F32),
            pltpu.VMEM((9 * mid, 128), F32),
            pltpu.VMEM((9 * s4, 128), F32),
            pltpu.VMEM(((strips - 2) * cols, wide), BF16),
            pltpu.VMEM((s4 // 128, (strips - 2) * cols, 128), F32),
            dma((1,)),
        ],
        compiler_params=limit(28),
        name="inner",
    )(scene, mids, spatial_bias[None], widen_bias[None], entry_bias[None], stride_bias[None], spatial_kernel, widen_kernel, entry_kernel.transpose(1, 2, 0), stride_kernel)

    operands = [last, beside, first, second, scene, w_reduce, b_reduce, mids, *kept, phases, three]
    three, four = pl.pallas_call(
        edge_kernel,
        out_shape=[
            jax.ShapeDtypeStruct((own, wide), BF16),
            jax.ShapeDtypeStruct((strips // 2 * half, s4), BF16),
        ],
        in_specs=[vmem] * (len(operands) - 1) + [hbm],
        out_specs=[hbm, vmem],
        input_output_aliases={len(operands) - 1: 0},
        scratch_shapes=[
            pltpu.VMEM((3, cols, 3 * mid), BF16),
            pltpu.VMEM((cols, wide), BF16),
            pltpu.VMEM((3 * cols, wide), BF16),
            pltpu.VMEM((s4 // 128, 3 * cols, 128), F32),
            pltpu.VMEM((3 * half, 3 * s4), BF16),
            dma((2,)),
        ],
        compiler_params=limit(28),
        name="edge",
    )(*operands)
    return three.reshape(strips, cols, wide), four.reshape(strips // 2, half, s4)


def solution(mesh):
    rows = P(("groups", "rows"), None, None)
    return jax.shard_map(shards, mesh=mesh, in_specs=(rows,) + (P(),) * 10, out_specs=(rows, rows), check_vma=False)
```

```python
import functools

import jax
import jax.numpy as jnp
from jax import lax
from jax.experimental import pallas as pl
from jax.experimental.pallas import tpu as pltpu
from jax.sharding import PartitionSpec as P

ORIENT = 8
BLOCK = 128
CYCLE_TAPS = [0, 1, 2, 5, 8, 7, 6, 3]
BF16, F32 = jnp.bfloat16, jnp.float32
NT = (((1,), (1,)), ((), ()))


def back_tap(tap, turn):
    if tap == 4:
        return 4
    return CYCLE_TAPS[(CYCLE_TAPS.index(tap) - turn) % ORIENT]


def iota(shape, dim):
    return lax.broadcasted_iota(jnp.int32, shape, dim)


def dot(a, b):
    return jnp.dot(a, b, preferred_element_type=F32)


def dot_nt(a, b):
    return lax.dot_general(a, b, NT, preferred_element_type=F32)


def rows_rolled(x, by):
    by %= x.shape[0]
    if by == 0:
        return x
    return jnp.concatenate([x[x.shape[0] - by:], x[:x.shape[0] - by]], 0)


def spread(fields, first, width):
    lead = iota((fields, width), 1) + first - ORIENT * iota((fields, width), 0)
    return jnp.where(lead & -ORIENT == 0, 1.0, 0.0).astype(BF16)


def turned(blocks, block):
    lane = iota((1, blocks.shape[1]), 1)
    for bit in (1, 2, 4):
        take = jnp.broadcast_to(lane & bit, blocks.shape) != 0
        blocks = jnp.where(take, rows_rolled(blocks, bit * block), blocks)
    return blocks


def unfold_in(tall_ref, kernel, fields, store):
    inputs = kernel.shape[1]
    base = jnp.concatenate([kernel[(-r) % ORIENT * fields:((-r) % ORIENT + 1) * fields] for r in range(ORIENT)], 0)
    base, other = base.T, rows_rolled(base, fields).T
    for first in range(0, inputs * ORIENT, 128):
        hot = tall_ref[pl.ds(first, 128), :]
        row = iota((128, fields * ORIENT), 0)
        block = jnp.where(row & 1 != 0, dot(hot, other), dot(hot, base))
        for bit in (2, 4):
            block = jnp.where(row & bit != 0, pltpu.roll(block, bit * fields, 1), block)
        store(pl.ds(first, 128), block.astype(BF16))


def bias_lanes(bias, hot):
    first = bias.astype(BF16)
    rest = bias - first.astype(F32)
    second = rest.astype(BF16)
    third = (rest - second.astype(F32)).astype(BF16)
    parts = [dot(jnp.broadcast_to(p, (16,) + p.shape[1:]), hot)[:1] for p in (first, second, third)]
    return parts[0] + parts[1] + parts[2]


def fetched(pairs, sem, first=0):
    copies = [pltpu.make_async_copy(source, target, sem.at[first + n]) for n, (source, target) in enumerate(pairs)]
    for copy in copies:
        copy.start()
    return copies


def shifted(y, cols):
    col = iota(y.shape, 0)
    left = jnp.where(col == 0, 0.0, pltpu.roll(y, 1, 0))
    right = jnp.where(col == cols - 1, 0.0, pltpu.roll(y, cols - 1, 0))
    return jnp.concatenate([left, y, right], 1).astype(BF16)


def tile_hot(fields, width):
    return jnp.where((iota((fields, width), 1) - iota((fields, width), 0)) & (fields - 1) == 0, 1.0, 0.0).astype(BF16)


def fetched(pairs, sem, first=0):
    copies = [pltpu.make_async_copy(source, target, sem.at[first + n]) for n, (source, target) in enumerate(pairs)]
    for copy in copies:
        copy.start()
    return copies


def load_kernel(x_hbm, last_ref, order_ref, tall_ref, flat_ref, sem):
    cols = last_ref.shape[0]
    copy = pltpu.make_async_copy(x_hbm.at[pl.ds(x_hbm.shape[0] - cols, cols)], last_ref, sem)
    copy.start()
    s4 = order_ref.shape[0]
    s4_f = s4 // ORIENT
    a, b = iota((s4, s4), 0), iota((s4, s4), 1)
    order_ref[...] = jnp.where(b == (a & (s4_f - 1)) * ORIENT + (a >> s4_f.bit_length() - 1), 1.0, 0.0).astype(BF16)
    flat_ref[...] = spread(flat_ref.shape[0], 0, flat_ref.shape[1])
    lead = iota(tall_ref.shape, 0) - ORIENT * iota(tall_ref.shape, 1)
    tall_ref[...] = jnp.where(lead & -ORIENT == 0, 1.0, 0.0).astype(BF16)
    copy.wait()


def reducing(tall_ref, xs_ref, kr_ref, br_ref, wr_ref, bias_ref, mids_ref, first_ref, second_ref):
    cols = first_ref.shape[0]
    strips = xs_ref.shape[0] // cols
    even = lax.axis_index("rows") % 2 == 0
    _, mid_f, in_f = kr_ref.shape
    def keep(at, block):
        wr_ref[at, :] = block
    unfold_in(tall_ref, kr_ref[...].reshape(mid_f * ORIENT, in_f), mid_f, keep)
    bias = bias_lanes(br_ref[...], tile_hot(mid_f, mid_f * ORIENT))
    bias_ref[...] = bias
    y = jnp.maximum(dot(xs_ref[...], wr_ref[...]) + bias, 0.0)
    parts = [y[row * cols:(row + 1) * cols] for row in range(strips)]
    first_ref[...] = jnp.where(even, parts[0], parts[strips - 2]).astype(BF16)
    second_ref[...] = jnp.where(even, parts[strips - 2], parts[0]).astype(BF16)
    for row, part in enumerate(parts):
        mids_ref[pl.ds(row * cols, cols), :] = shifted(part, cols)


def strip_blocks(jobs, ws_ref, ww_ref, b_mid, b_wid, threes):
    twos = []
    for windows, _, _ in jobs:
        depth = windows[0].shape[1]
        acc = b_mid
        for dy in range(3):
            acc = acc + dot(windows[dy], ws_ref[pl.ds(dy * depth, depth), :])
        twos.append(jnp.maximum(acc, 0.0).astype(BF16))
    for two, (_, x, at) in zip(twos, jobs):
        for first in range(0, ww_ref.shape[1], 256):
            part = slice(first, first + 256)
            z = x(part).astype(F32) + dot(two, ww_ref[:, part]) + b_wid[:, part]
            threes[at, part] = jnp.maximum(z, 0.0).astype(BF16)


def entry_part(threes, we_ref, b_ent, at, first):
    cut = slice(first, first + 256)
    return jnp.maximum(dot(threes[at, :], we_ref[:, cut]) + b_ent[:, cut], 0.0)


def thirds(fours, threes, we_ref, b_ent, scales, cols, phases):
    half = cols // 2
    s4 = we_ref.shape[1]
    for first in range(0, s4, 256):
        for strip, scale in enumerate(scales):
            f = entry_part(threes, we_ref, b_ent, pl.ds(strip * cols, cols), first)
            if scale is not None:
                f = f * scale
            for g in range(2):
                fours[first // 128 + g, pl.ds(strip * cols, cols), :] = f[:, g * 128:(g + 1) * 128]
    col = iota((half, 128), 0)
    for strip in range(len(scales)):
        for g in range(s4 // 128):
            even = fours[g, pl.ds(strip * cols, half, stride=2), :]
            odd = fours[g, pl.ds(strip * cols + 1, half, stride=2), :]
            moved = jnp.where(col == 0, 0.0, pltpu.roll(odd, 1, 0))
            for n, value in enumerate((moved, even, odd)):
                phases[pl.ds(strip * half, half), pl.ds(n * s4 + g * 128, 128)] = value.astype(BF16)


def inner_kernel(tall_ref, flat_ref, xs_ref, mids_ref, bs_ref, bw_ref, be_ref, bt_ref, ks_v, kw_ref, ke_ref, kt_v,
                 three_ref, ws_ref, ww_ref, we_ref, k2_ref, b_mid_ref, b_wid_ref, b_ent_ref, b_str_ref, phases_ref,
                 flat_w, flat_s, flat_t, threes, fours, sem):
    in_f, s4_f, mid_f = ke_ref.shape[2], ke_ref.shape[1], kw_ref.shape[0]
    wide, s4, mid = in_f * ORIENT, s4_f * ORIENT, mid_f * ORIENT
    cols = phases_ref.shape[0]
    strips = xs_ref.shape[0] // cols
    flat_w[...] = kw_ref[...].astype(F32).reshape(mid, in_f)
    kw = jnp.concatenate([flat_w[pl.ds(u, mid_f, stride=ORIENT), :] for u in range(ORIENT)], 0).astype(BF16)
    hot_s4 = tile_hot(s4_f, s4)
    b_mid_ref[...] = bias_lanes(bs_ref[...], tile_hot(mid_f, mid))
    b_ent_ref[...] = bias_lanes(be_ref[...], hot_s4)
    b_str_ref[...] = bias_lanes(bt_ref[...], hot_s4)
    for first in range(0, wide, 256):
        hot = flat_ref[:, pl.ds(first, 256)]
        ww_ref[:, pl.ds(first, 256)] = turned(dot(kw, hot), mid_f).astype(BF16)
        b_wid_ref[:, pl.ds(first, 256)] = bias_lanes(bw_ref[...], hot)
    def keep(at, block):
        we_ref[at, :] = block
    unfold_in(tall_ref, ke_ref[...].reshape(s4, in_f), s4_f, keep)

    lane = iota((1, 128), 1)
    for tap in range(9):
        flat_s[pl.ds(tap * mid, mid), :mid_f] = ks_v[tap].astype(F32).reshape(mid, mid_f)
    piece = lambda tap, u: flat_s[pl.ds(tap * mid + u % ORIENT, mid_f, stride=ORIENT), :]
    low = jnp.broadcast_to(lane < mid_f, (mid_f, 128))
    half = jnp.broadcast_to(lane < 2 * mid_f, (mid_f, 128))
    pairs = {}
    for tap in range(9):
        for u in range(ORIENT):
            pairs[tap, u] = jnp.where(low, piece(tap, u), pltpu.roll(piece(back_tap(tap, 1), u - 1), mid_f, 1))
    for tap in range(9):
        for u in range(ORIENT):
            quad = jnp.where(half, pairs[tap, u], pltpu.roll(pairs[back_tap(tap, 2), (u - 2) % ORIENT], 2 * mid_f, 1)).astype(BF16)
            ws_ref[pl.ds(tap * mid + u * mid_f, mid_f), :128] = quad
            ahead = back_tap(tap, -4)
            ws_ref[pl.ds(ahead * mid + (u + 4) % ORIENT * mid_f, mid_f), 128:] = quad

    for tap in range(9):
        flat_t[pl.ds(tap * s4, s4), :s4_f] = kt_v[tap].astype(F32).reshape(s4, s4_f)
    piece_t = lambda tap, u: flat_t[pl.ds(tap * s4 + u % ORIENT, s4_f, stride=ORIENT), :]
    low_t = jnp.broadcast_to(lane < s4_f, (s4_f, 128))
    for tap in range(9):
        for u in range(ORIENT):
            pair = jnp.where(low_t, piece_t(tap, u), pltpu.roll(piece_t(back_tap(tap, 1), u - 1), s4_f, 1))
            k2_ref[pl.ds(tap * s4 + u * s4_f, s4_f), :] = pair.astype(BF16)

    inner = strips - 2
    strip_of = lambda row: mids_ref[pl.ds(row * cols, cols), :]
    jobs = [([strip_of(row + dy) for dy in range(3)], lambda part, row=row: xs_ref[pl.ds((row + 1) * cols, cols), part],
             pl.ds(row * cols, cols)) for row in range(inner)]
    strip_blocks(jobs, ws_ref, ww_ref, b_mid_ref[...], b_wid_ref[...], threes)
    out = pltpu.make_async_copy(threes, three_ref.at[pl.ds(cols, inner * cols)], sem.at[0])
    out.start()
    thirds(fours, threes, we_ref, b_ent_ref[...], [None] * inner, cols, phases_ref)
    out.wait()


def edge_kernel(last_ref, beside_ref, first_ref, second_ref, xs_ref, wr_ref, bias_ref, order_ref, mids_ref, ws_ref, ww_ref, we_ref, k2_ref,
                b_mid_ref, b_wid_ref, b_ent_ref, b_str_ref, inner_ref, kept_ref,
                three_ref, four_ref, halo, line, threes, fours, phases, sem):
    place, count = lax.axis_index("rows"), lax.axis_size("rows")
    even = lax.axis_index("rows") % 2 == 0
    cols = first_ref.shape[0]
    half = cols // 2
    strips = xs_ref.shape[0] // cols
    wide, mid, s4 = xs_ref.shape[1], wr_ref.shape[1], we_ref.shape[1]
    not_first = jnp.where(place == 0, 0.0, 1.0)
    not_last = jnp.where(place == count - 1, 0.0, 1.0)
    strip_of = lambda row: mids_ref[pl.ds(row * cols, cols), :]
    line[...] = jnp.where(even, last_ref[...], beside_ref[...])
    got = [first_ref[...].astype(F32), second_ref[...].astype(F32)]
    last = strips - 1
    b_mid, b_wid, b_ent = b_mid_ref[...], b_wid_ref[...], b_ent_ref[...]
    halo[0] = shifted(jnp.where(even, got[0], got[1]) * not_first, cols)
    halo[2] = shifted(jnp.where(even, got[1], got[0]) * not_last, cols)
    halo[1] = shifted(jnp.maximum(dot(line[...], wr_ref[...]) + bias_ref[...], 0.0) * not_first, cols)
    below = [strip_of(0), strip_of(1)] if last > 1 else [strip_of(0), halo[2]]
    jobs = [
        ([halo[0], halo[1], strip_of(0)], lambda part: line[:, part], pl.ds(0, cols)),
        ([halo[1], *below], lambda part: xs_ref[pl.ds(0, cols), part], pl.ds(cols, cols)),
        ([strip_of(last - 1), strip_of(last), halo[2]], lambda part: xs_ref[pl.ds(last * cols, cols), part], pl.ds(2 * cols, cols)),
    ]
    strip_blocks(jobs, ws_ref, ww_ref, b_mid, b_wid, threes)
    outs = [
        pltpu.make_async_copy(threes.at[pl.ds(cols, cols)], three_ref.at[pl.ds(0, cols)], sem.at[0]),
        pltpu.make_async_copy(threes.at[pl.ds(2 * cols, cols)], three_ref.at[pl.ds(last * cols, cols)], sem.at[1]),
    ]
    for out in outs:
        out.start()
    thirds(fours, threes, we_ref, b_ent, [not_first, None, None], cols, phases)

    def rows_of(row, dx):
        cut = slice(dx * s4, (dx + 1) * s4)
        if row < 1:
            return phases[pl.ds((row + 1) * half, half), cut]
        if row == last:
            return phases[pl.ds(2 * half, half), cut]
        return inner_ref[pl.ds((row - 1) * half, half), cut]

    def filter_tile(tap, pair):
        halves = []
        for j in (2 * pair, 2 * pair + 1):
            source = back_tap(tap, 2 * j)
            halves.append(rows_rolled(k2_ref[pl.ds(source * s4, s4), :], 128 * j))
        return jnp.concatenate(halves, 1)

    lhs = []
    for tap in range(9):
        dy, dx = divmod(tap, 3)
        lhs.append(jnp.concatenate([rows_of(2 * q + dy - 1, dx) for q in range(strips // 2)], 0))
    results = []
    for pair in range(s4 // 256):
        acc = b_str_ref[:, pair * 256:(pair + 1) * 256]
        for tap in range(9):
            acc = acc + dot(lhs[tap], filter_tile(tap, pair))
        results.append(jnp.maximum(acc, 0.0).astype(BF16))
    four_ref[...] = dot(jnp.concatenate(results, 1), order_ref[...]).astype(BF16)
    for out in outs:
        out.wait()


def swaps(groups, count):
    near, far = [], []
    for group in range(groups):
        for row in range(count):
            me = group * count + row
            if row ^ 1 < count:
                near.append((me, group * count + (row ^ 1)))
            other = row - 1 if row % 2 == 0 else row + 1
            if 0 <= other < count:
                far.append((me, group * count + other))
            elif group ^ 1 < groups:
                far.append((me, (group ^ 1) * count + row))
    return near, far


def odd_down(count):
    if count < 8 or count % 4:
        return [(i, (i + 1) % count) for i in range(count)]
    pairs = {i: i + 1 for i in range(count - 1)}
    for i in range(2, count - 4, 4):
        pairs[i] = i - 3 if i > 2 else 0
    pairs[count - 1] = count - 5
    return sorted(pairs.items())


def shards(scene_map, reduce_kernel, reduce_bias, spatial_kernel, spatial_bias, widen_kernel, widen_bias,
           entry_kernel, entry_bias, stride_kernel, stride_bias):
    count = lax.axis_size("rows")
    strips, cols, wide = scene_map.shape
    mid_f, s4_f = reduce_kernel.shape[2], entry_kernel.shape[2]
    mid, s4 = mid_f * ORIENT, s4_f * ORIENT
    own, half = strips * cols, cols // 2
    hbm = pl.BlockSpec(memory_space=pl.ANY)
    vmem = pl.BlockSpec(memory_space=pltpu.VMEM)
    dma = pltpu.SemaphoreType.DMA
    limit = lambda mib: pltpu.CompilerParams(vmem_limit_bytes=mib << 20)

    pinned = lambda *arrays: [pltpu.with_memory_space_constraint(a, pltpu.HBM) for a in arrays]
    scene = scene_map.reshape(own, wide)
    work = lambda flops: pl.CostEstimate(flops=flops, transcendentals=0, bytes_accessed=1 << 22)
    last, order, tall, wide_hot = pl.pallas_call(
        load_kernel,
        out_shape=[
            pltpu.VMEM((cols, wide), BF16),
            pltpu.VMEM((s4, s4), BF16),
            pltpu.VMEM((wide, wide // ORIENT), BF16),
            pltpu.VMEM((wide // ORIENT, wide), BF16),
        ],
        in_specs=[hbm],
        out_specs=[vmem] * 4,
        scratch_shapes=[dma],
        cost_estimate=work(2 * 10**9),
        compiler_params=limit(16),
        name="load",
    )(*pinned(scene))
    near, far = swaps(lax.axis_size("groups"), count)
    beside = lax.ppermute(last, ("groups", "rows"), near)
    last = lax.ppermute(last, "rows", odd_down(count))
    w_reduce, b_reduce, mids, first, second = pl.pallas_call(
        reducing,
        out_shape=[
            pltpu.VMEM((wide, mid), BF16),
            pltpu.VMEM((1, mid), F32),
            pltpu.VMEM((own, 3 * mid), BF16),
            pltpu.VMEM((cols, mid), BF16),
            pltpu.VMEM((cols, mid), BF16),
        ],
        in_specs=[vmem] * 4,
        out_specs=[vmem] * 5,
        cost_estimate=work(2 * 10**9),
        compiler_params=limit(16),
        name="reduce",
    )(tall, scene, reduce_kernel.transpose(1, 2, 0), reduce_bias[None])
    first = lax.ppermute(first, ("groups", "rows"), far)
    second = lax.ppermute(second, ("groups", "rows"), near)

    three, *kept, phases = pl.pallas_call(
        inner_kernel,
        out_shape=[
            jax.ShapeDtypeStruct((own, wide), BF16),
            pltpu.VMEM((9 * mid, mid), BF16),
            pltpu.VMEM((mid, wide), BF16),
            pltpu.VMEM((wide, s4), BF16),
            pltpu.VMEM((9 * s4, 128), BF16),
            pltpu.VMEM((1, mid), F32),
            pltpu.VMEM((1, wide), F32),
            pltpu.VMEM((1, s4), F32),
            pltpu.VMEM((1, s4), F32),
            pltpu.VMEM(((strips - 2) * half, 3 * s4), BF16),
        ],
        in_specs=[vmem] * 12,
        out_specs=[hbm] + [vmem] * 9,
        scratch_shapes=[
            pltpu.VMEM((mid, wide // ORIENT), F32),
            pltpu.VMEM((9 * mid, 128), F32),
            pltpu.VMEM((9 * s4, 128), F32),
            pltpu.VMEM(((strips - 2) * cols, wide), BF16),
            pltpu.VMEM((s4 // 128, (strips - 2) * cols, 128), F32),
            dma((1,)),
        ],
        compiler_params=limit(28),
        name="inner",
    )(tall, wide_hot, scene, mids, spatial_bias[None], widen_bias[None], entry_bias[None], stride_bias[None], spatial_kernel, widen_kernel, entry_kernel.transpose(1, 2, 0), stride_kernel)

    operands = [last, beside, first, second, scene, w_reduce, b_reduce, order, mids, *kept, phases, three]
    three, four = pl.pallas_call(
        edge_kernel,
        out_shape=[
            jax.ShapeDtypeStruct((own, wide), BF16),
            jax.ShapeDtypeStruct((strips // 2 * half, s4), BF16),
        ],
        in_specs=[vmem] * (len(operands) - 1) + [hbm],
        out_specs=[hbm, vmem],
        input_output_aliases={len(operands) - 1: 0},
        scratch_shapes=[
            pltpu.VMEM((3, cols, 3 * mid), BF16),
            pltpu.VMEM((cols, wide), BF16),
            pltpu.VMEM((3 * cols, wide), BF16),
            pltpu.VMEM((s4 // 128, 3 * cols, 128), F32),
            pltpu.VMEM((3 * half, 3 * s4), BF16),
            dma((2,)),
        ],
        compiler_params=limit(28),
        name="edge",
    )(*operands)
    return three.reshape(strips, cols, wide), four.reshape(strips // 2, half, s4)


def solution(mesh):
    rows = P(("groups", "rows"), None, None)
    return jax.shard_map(shards, mesh=mesh, in_specs=(rows,) + (P(),) * 10, out_specs=(rows, rows), check_vma=False)
```
